32 devices in a mesh: grp: 4 (over y, core), dev: 8 (over z, x).
Axes of the slice: x: 2, y: 2, z: 4, core: 2. Of those that a mesh axis runs over, the one named last changes fastest.
Arguments:
- u_blocks: float32 [768, 32, 1024], P(('grp', 'dev')), may hold values from -20 to 20
- v_blocks: float32 [768, 32, 1024], P(('grp', 'dev')), may hold values from -0.1875 to 0.1875
- sketch: float32 [64, 32, 1024], P(('grp', 'dev')), may hold values from -6 to 6
- near_diag: float32 [64, 1024], P(('grp', 'dev')), may hold values from 0.3 to 72
- block_row: int32 [768], P(('grp', 'dev')), may hold values from 0 to 15, as said below
- col_count: int32 [64], P(('grp', 'dev')), may hold values from 8 to 12, as said below
Outputs:
- leaf_basis: float32 [64, 32, 1024], P(('grp', 'dev'))
- transfer_leaf: float32 [64, 32, 32], P(('grp', 'dev'))
- transfer_group: float32 [4, 32, 32], P('grp')
The draws below stay inside these ranges and needn't reach their ends.
Inputs may be any that keep to these rules, and one draw needn't show every extreme that they name: A device's slots hold its blocks in the order of its column clusters, col_count[c] of them for cluster c; the remaining slots are empty. The row cluster block_row[s] belongs to device block_row[s] // 2 of the same subtree. Among the live slots of one device at most 3 have row clusters of any one device, and in every subtree some device is named by exactly 3 live slots of every device of that subtree.
All inputs are finite; a program needn't handle non-finite values.
Results may differ from the reference program's by a relative error of at most 0.0003.
Values sent between devices are 32-bit elements; how exact they have to be, the bound alone decides.
A program may use at most 128 MiB of HBM per device.

```python
import math
import jax
import jax.numpy as jnp
from jax import lax

R = 32
LEAF = 1024
L_DEV = 2
CMIN = 8
CMAX = 12
MEMBERS = 8
GROUPS = 4
CAP = 3
BLK_DEV = 24
CLUSTERS = 64
NBLK = 768


def route_plan(key):
    base_key = jax.random.fold_in(key, 4242)
    key_count, key_busy, key_pool, key_front, key_local = jax.random.split(base_key, 5)
    devices_all = GROUPS * MEMBERS
    counts = jax.random.randint(key_count, (devices_all * L_DEV,), CMIN, CMAX + 1).astype(jnp.int32)
    busy_group = jax.random.randint(key_busy, (GROUPS,), 0, MEMBERS).astype(jnp.int32)
    busy_dev = jnp.repeat(busy_group, MEMBERS)
    others = (busy_dev[:, None] + 1 + jnp.arange(MEMBERS - 1, dtype=jnp.int32)[None, :]) % MEMBERS
    spread = jnp.repeat(others, CAP, axis=1)
    pool_keys = jax.random.split(key_pool, devices_all)
    shuffled = jax.vmap(jax.random.permutation)(pool_keys, spread)
    pool = jnp.concatenate([jnp.repeat(busy_dev[:, None], CAP, axis=1), shuffled], axis=1)[:, :BLK_DEV]
    front_len = L_DEV * CMIN
    front_keys = jax.random.split(key_front, devices_all)
    front_order = jax.vmap(lambda key_one: jax.random.permutation(key_one, front_len))(front_keys)
    head_part = jnp.take_along_axis(pool[:, :front_len], front_order, axis=1)
    pool = jnp.concatenate([head_part, pool[:, front_len:]], axis=1)
    local_ids = jax.random.randint(key_local, (devices_all, BLK_DEV), 0, L_DEV).astype(jnp.int32)
    row_ids = (pool * L_DEV + local_ids).astype(jnp.int32)
    return (counts, row_ids.reshape(-1))


def rise_of(owner_dev, group_ids):
    return (1.0 + 2.0 * owner_dev / max(MEMBERS - 1, 1)) * (1.0 + 2.0 * group_ids / max(GROUPS - 1, 1))


def draw_block_row(key, part):
    return route_plan(key)[1]


def draw_col_count(key, part):
    return route_plan(key)[0]


def draw_u_blocks(key, part):
    counts, row_ids = route_plan(key)
    block_total = GROUPS * MEMBERS * BLK_DEV
    key_entries, key_scale = jax.random.split(jax.random.fold_in(key, 99))
    owner_dev = (row_ids // L_DEV).astype(jnp.float32)
    group_ids = (jnp.arange(block_total) // (BLK_DEV * MEMBERS)).astype(jnp.float32)
    rise_factor = rise_of(owner_dev, group_ids)
    entries = jax.random.truncated_normal(key_entries, -4.0, 4.0, (block_total, R, LEAF), jnp.float32)
    block_scale = jnp.exp(jax.random.uniform(key_scale, (block_total,), jnp.float32, math.log(0.5), math.log(2.0)))
    return entries * (rise_factor * block_scale)[:, None, None] / math.sqrt(R)


def draw_near_diag(key, part):
    key_values = jax.random.fold_in(key, 77)
    cluster_ids = jnp.arange(CLUSTERS)
    group_ids = (cluster_ids // (MEMBERS * L_DEV)).astype(jnp.float32)
    owner_dev = (cluster_ids % (MEMBERS * L_DEV) // L_DEV).astype(jnp.float32)
    rise_factor = rise_of(owner_dev, group_ids)
    values = jnp.exp(jax.random.uniform(key_values, (CLUSTERS, LEAF), jnp.float32, math.log(0.5), math.log(5.0)))
    return values * rise_factor[:, None]


def level_of(key, extent, shards, low, high):
    loudness, own = 1.0, jax.random.fold_in(key, 6)
    for position, parts in shards:
        steps = jnp.exp(jax.random.uniform(jax.random.fold_in(own, position), (parts,), jnp.float32, low / len(shards), high / len(shards)))
        loudness = loudness * jnp.repeat(steps, extent[position] // parts).reshape([-1 if axis == position else 1 for axis in range(len(extent))])
    return loudness


def noise(own_key, dims, deviation, reach, shards=(), kind=jnp.bfloat16):
    loudness = level_of(own_key, dims, shards, -0.22, 0.18) if shards else 1.0
    drawn = jax.random.normal(own_key, dims, jnp.float32) * deviation * loudness
    return jnp.minimum(jnp.maximum(drawn, -reach), reach).astype(kind)


def setup_inputs(seed: int = 0) -> dict:
    key_list = jax.random.split(jax.random.key(seed), 7)
    return {
        "u_blocks": draw_u_blocks(jax.random.fold_in(key_list[6], 71), 0),
        "v_blocks": noise(key_list[1], (NBLK, R, LEAF), LEAF ** -0.5, 0.1875, ((0, 32),), jnp.float32),
        "sketch": noise(key_list[2], (CLUSTERS, R, LEAF), 1.0, 6.0, ((0, 32),), jnp.float32),
        "near_diag": draw_near_diag(jax.random.fold_in(key_list[6], 71), 0),
        "block_row": draw_block_row(jax.random.fold_in(key_list[6], 71), 0),
        "col_count": draw_col_count(jax.random.fold_in(key_list[6], 71), 0),
    }


def positive_qr(stacked):
    q_factor, r_factor = jnp.linalg.qr(stacked)
    sign_flip = jnp.sign(jnp.diagonal(r_factor, axis1=-2, axis2=-1))
    return (q_factor * sign_flip[..., None, :], r_factor * sign_flip[..., :, None])

def reference(u_blocks, v_blocks, sketch, near_diag, block_row, col_count):
    highest = lax.Precision.HIGHEST
    devices_all = GROUPS * MEMBERS
    counts = col_count.reshape(devices_all, L_DEV)
    slot_ends = jnp.cumsum(counts, axis=1)
    slot_index = jnp.arange(BLK_DEV, dtype=jnp.int32)
    alive_slot = slot_index[None, :] < slot_ends[:, -1:]
    col_local = jnp.minimum(lax.optimization_barrier(jnp.sum((slot_ends[:, None, :] <= slot_index[None, :, None]).astype(jnp.int32), axis=2)), L_DEV - 1)
    device_ids = jnp.arange(devices_all, dtype=jnp.int32)[:, None]
    col_ids = (device_ids * L_DEV + col_local).astype(jnp.int32)
    row_ids = (device_ids // MEMBERS * (MEMBERS * L_DEV) + block_row.reshape(devices_all, BLK_DEV)).astype(jnp.int32)

    def accumulate(running, pieces):
        u_part, v_part, col_part, row_part, alive_part = pieces
        picked = sketch[col_part]
        coupling = jnp.einsum('bkl,bml->bkm', v_part, picked, precision=highest)
        coupling = jnp.where(alive_part[:, None, None], coupling, 0.0)
        contribution = jnp.einsum('bkm,bkl->bml', coupling, u_part, precision=highest)
        return (running.at[row_part].add(contribution), None)
    initial = jnp.zeros(sketch.shape, jnp.float32)
    far_sample, _ = lax.scan(accumulate, initial, (u_blocks.reshape(devices_all, BLK_DEV, R, LEAF), v_blocks.reshape(devices_all, BLK_DEV, R, LEAF), col_ids, row_ids, alive_slot))
    sample = far_sample + near_diag[:, None, :] * sketch
    q_leaf, r_leaf = positive_qr(jnp.swapaxes(sample, 1, 2))
    leaf_basis = jnp.swapaxes(q_leaf, 1, 2) * math.sqrt(LEAF)
    q_group, r_group = positive_qr(r_leaf.reshape(GROUPS, MEMBERS * L_DEV * R, R))
    transfer_leaf = q_group.reshape(CLUSTERS, R, R) * math.sqrt(MEMBERS * L_DEV)
    q_root, r_root = positive_qr(r_group.reshape(GROUPS * R, R))
    transfer_group = q_root.reshape(GROUPS, R, R) * math.sqrt(GROUPS)
    return (leaf_basis, transfer_leaf, transfer_group)
```

```python
import functools
import math

import jax
import jax.numpy as jnp
from jax import lax
from jax.experimental import pallas as pl
from jax.experimental.pallas import tpu as pltpu
from jax.sharding import PartitionSpec as P

F32 = jnp.float32
BF16 = jnp.bfloat16
MESH = pl.DeviceIdType.MESH
HIGHEST = lax.Precision.HIGHEST
NN = (((1,), (0,)), ((), ()))
NT = (((1,), (1,)), ((), ()))
WIDTH = 128
PAIR = 2
V_PARTS = 3


def dot(a, b, dims, precision=None):
    return lax.dot_general(a, b, dims, precision=precision, preferred_element_type=F32)


def split(x):
    high = x.astype(BF16)
    return high, (x - high.astype(F32)).astype(BF16)


def dot3(a, b, dims):
    (ah, al), (bh, bl) = a, b
    return dot(ah, bh, dims) + dot(ah, bl, dims) + dot(al, bh, dims)


def pack(square):
    rank = square.shape[0]
    return jnp.concatenate([square[i : i + 8] for i in range(0, rank, 8)], axis=1)


def unpack(packed, rank):
    return jnp.concatenate([packed[:, i * rank : (i + 1) * rank] for i in range(rank // 8)], axis=0)


def diagonal_block(square, c, rank):
    at = slice(c * rank, (c + 1) * rank)
    return square[at, at]


def factor(grams):
    rank = grams[0].shape[0]
    rows = lax.broadcasted_iota(jnp.int32, (rank, 2 * rank), 0)
    lanes = lax.broadcasted_iota(jnp.int32, (rank, 2 * rank), 1)
    eye = (
        lax.broadcasted_iota(jnp.int32, (rank, rank), 0)
        == lax.broadcasted_iota(jnp.int32, (rank, rank), 1)
    ).astype(F32)
    state = [jnp.concatenate([g, eye], axis=1) for g in grams]
    for j in range(rank - 1):
        below = rows > j
        for n, m in enumerate(state):
            column = jnp.broadcast_to(m[:, j : j + 1], m.shape)
            scaled = m[j : j + 1, :] / column[j : j + 1, :]
            state[n] = m - jnp.where(below, column, 0.0) * scaled
    out = []
    for m in state:
        diagonal = jnp.sum(jnp.where(rows == lanes, m, 0.0), axis=1, keepdims=True)
        m = m * lax.rsqrt(diagonal)
        upper = jnp.where((rows <= lanes)[:, :rank], m[:, :rank], 0.0)
        out.append((upper, m[:, rank:]))
    return out


def kernel(
    xs, local, u_hbm, v_hbm, sketch_hbm, diag_hbm, block_row, col_count, sample_out, gram_out, sums_out,
    sketch, diag, u_buf, v_buf, u_high, u_low, w_high, w_low, part, got_x, got_mate, got_far, sample,
    gram, grams, group_gram, group_grams,
    load_sems, x_send, x_recv, m_send, m_recv, f_send, f_recv, g_send, g_recv, r_send, r_recv, relay,
):
    slots, leaf_rows = u_buf.shape
    rank = sample.shape[0] // local
    blocks = slots // rank
    members = grams.shape[0]
    groups = group_grams.shape[0]
    zs = members // xs
    chunks = leaf_rows // WIDTH
    own_rows = local * rank
    me = lax.axis_index("dev")
    my_group = lax.axis_index("grp")
    z, x = me // xs, me % xs

    pairs = chunks // PAIR
    near_loads = [
        pltpu.make_async_copy(sketch_hbm, sketch, load_sems.at[0]),
        pltpu.make_async_copy(diag_hbm, diag, load_sems.at[1]),
    ]
    v_rows = slots // V_PARTS
    v_loads = [
        pltpu.make_async_copy(
            v_hbm.at[pl.ds(i * v_rows, v_rows)],
            v_buf.at[pl.ds(i * v_rows, v_rows)],
            load_sems.at[2 + i],
        )
        for i in range(V_PARTS)
    ]
    u_loads = []
    for p in range(pairs):
        at = pl.ds(p * PAIR * WIDTH, PAIR * WIDTH)
        u_loads.append(
            pltpu.make_async_copy(
                u_hbm.at[:, at], u_buf.at[:, at], load_sems.at[2 + V_PARTS + p]
            )
        )
    for load in near_loads[:1] + v_loads + u_loads + near_loads[1:]:
        load.start()
    barrier = pltpu.get_barrier_semaphore()
    for xo in range(1, xs):
        partner = z * xs + (x + xo) % xs
        pl.semaphore_signal(barrier, inc=1, device_id={"dev": partner}, device_id_type=MESH)
    for o in range(1, groups):
        pl.semaphore_signal(
            barrier, inc=1, device_id={"grp": (my_group + o) % groups}, device_id_type=MESH
        )

    def greet(semaphore):
        @pl.when(z > 0)
        def _():
            pl.semaphore_signal(
                semaphore, inc=1, device_id={"dev": me - xs}, device_id_type=MESH
            )

        @pl.when(z < zs - 1)
        def _():
            pl.semaphore_signal(
                semaphore, inc=1, device_id={"dev": me + xs}, device_id_type=MESH
            )

    team = 2 if zs % 2 == 0 else 1
    first, seat = z // team * team, z % team
    teams = zs // team

    def peer_z(k):
        if k == 0:
            return z
        if k < team:
            return first + (seat + k) % team
        return (first + k) % zs

    order = list(range(team, zs)) + list(range(1, team))
    near_z = jnp.where(z > 0, 1, 0) + jnp.where(z < zs - 1, 1, 0)
    greet(barrier)

    lane = lax.broadcasted_iota(jnp.int32, (1, slots), 1)
    row_of = jnp.zeros((1, slots), jnp.int32)
    slot_of = jnp.zeros((1, slots), jnp.int32)
    for s in range(blocks):
        row_of = jnp.where(lane >= s * rank, block_row[s], row_of)
        slot_of = jnp.where(lane >= s * rank, s, slot_of)
    col_of = jnp.zeros((1, slots), jnp.int32)
    end = 0
    for c in range(local):
        end = end + col_count[c]
        col_of = col_of + jnp.where(slot_of >= end, 1, 0)

    near_loads[0].wait()
    sketch_parts = split(sketch[...])
    parts = []
    for i in range(V_PARTS):
        v_loads[i].wait()
        parts.append(dot3(sketch_parts, split(v_buf[i * v_rows : (i + 1) * v_rows]), NT))
    every = jnp.concatenate(parts, axis=1)
    coupling = jnp.zeros((rank, slots), F32)
    for c in range(local):
        coupling = coupling + jnp.where(col_of == c, every[c * rank : (c + 1) * rank], 0.0)
    high, low = (part_.astype(F32) for part_ in split(coupling))

    def place(xo):
        for zo in range(zs):
            dest = peer_z(zo) * xs + (x + xo) % xs
            for c in range(local):
                hit = row_of == dest * local + c
                at = pl.ds((zo * local + c) * rank, rank)
                w_high[xo, at, :] = jnp.where(hit, high, 0.0).astype(BF16)
                w_low[xo, at, :] = jnp.where(hit, low, 0.0).astype(BF16)

    for xo in range(1, xs):
        place(xo)

    def contribute(xo, p):
        at = pl.ds(p * PAIR * WIDTH, PAIR * WIDTH)
        out = dot3((w_high[xo], w_low[xo]), (u_high[:, at], u_low[:, at]), NN)
        for h in range(PAIR):
            part[xo, p * PAIR + h] = out[:, h * WIDTH : (h + 1) * WIDTH]

    def x_copy(xo, q, k):
        at = pl.ds(k * own_rows, own_rows)
        return pltpu.make_async_remote_copy(
            src_ref=part.at[xo, q, at],
            dst_ref=got_x.at[xo - 1, q, at],
            send_sem=x_send.at[xo - 1, q, k],
            recv_sem=x_recv.at[xo - 1, q, k],
            device_id={"dev": z * xs + (x + xo) % xs},
            device_id_type=MESH,
        )

    def block(k):
        return pl.ds(k * own_rows, own_rows)

    def mate_copy(k, q):
        return pltpu.make_async_remote_copy(
            src_ref=part.at[0, q, block(k)],
            dst_ref=got_mate.at[k - 1, q],
            send_sem=m_send.at[k - 1, q],
            recv_sem=m_recv.at[k - 1, q],
            device_id={"dev": (first + team - 1 - seat) * xs + x},
            device_id_type=MESH,
        )

    def far_copy(k, q):
        slot = teams - k // team - 1
        return pltpu.make_async_remote_copy(
            src_ref=part.at[0, q, block(k)],
            dst_ref=got_far.at[slot, q],
            send_sem=f_send.at[k - team, q],
            recv_sem=f_recv.at[slot, q],
            device_id={"dev": peer_z(k) * xs + x},
            device_id_type=MESH,
        )

    def hands_over(k):
        return jnp.where(first + k < zs, 0, 1) == seat

    def pass_on(hop):
        pl.semaphore_wait(relay.at[hop], near_z)
        if hop < zs - 2:
            greet(relay.at[hop + 1])

    for p in range(pairs):
        at = pl.ds(p * PAIR * WIDTH, PAIR * WIDTH)
        u_loads[p].wait()
        u_high[:, at], u_low[:, at] = split(u_buf[:, at])
        for xo in range(1, xs):
            contribute(xo, p)
        if p == 0:
            pl.semaphore_wait(barrier, xs - 1 + groups - 1 + near_z)
            greet(relay.at[0])
        for q in range(p * PAIR, (p + 1) * PAIR):
            for k in order:
                for xo in range(1, xs):
                    x_copy(xo, q, k).start()
        if 1 <= p < zs:
            pass_on(p - 1)
    for q in range(chunks):
        for xo in range(1, xs):
            x_copy(xo, q, 0).start()
    for hop in range(min(pairs - 1, zs - 1), zs - 1):
        pass_on(hop)
    place(0)

    def gather(k, q):
        total = part[0, q, block(k)]
        for xo in range(1, xs):
            x_copy(xo, q, k).wait_recv()
            total = total + got_x[xo - 1, q, block(k)]
        return total

    for p in range(pairs):
        contribute(0, p)
        for q in range(p * PAIR, (p + 1) * PAIR):
            for k in order:
                part[0, q, block(k)] = gather(k, q)
                if k < team:
                    mate_copy(k, q).start()
                elif team > 1:
                    @pl.when(hands_over(k))
                    def _(k=k, q=q):
                        mate_copy(k, q).start()
            for k in range(team, zs):
                def send_far(k=k, q=q):
                    if team > 1:
                        mate_copy(k, q).wait_recv()
                        part[0, q, block(k)] = part[0, q, block(k)] + got_mate[k - 1, q]
                    far_copy(k, q).start()

                if team > 1:
                    pl.when(jnp.logical_not(hands_over(k)))(send_far)
                else:
                    send_far()
    near_loads[1].wait()
    leaf_gram = jnp.zeros((own_rows, own_rows), F32)
    for q in range(chunks):
        at = pl.ds(q * WIDTH, WIDTH)
        near = [
            diag[c : c + 1, at] * sketch[c * rank : (c + 1) * rank, at] for c in range(local)
        ]
        total = gather(0, q) + jnp.concatenate(near, axis=0)
        for k in range(1, team):
            mate_copy(k, q).wait_recv()
            total = total + got_mate[k - 1, q]
        for k in range(team, zs, team):
            slot = teams - k // team - 1
            far_copy(k, q).wait_recv()
            total = total + got_far[slot, q]
        sample[:, at] = total
        leaf_gram = leaf_gram + dot(total, total, NT, HIGHEST)

    save = pltpu.make_async_copy(sample, sample_out, load_sems.at[0])
    save.start()
    gram_out[...] = leaf_gram
    packed = pack(
        functools.reduce(jnp.add, [diagonal_block(leaf_gram, c, rank) for c in range(local)])
    )
    gram[...] = packed
    grams[pl.ds(me, 1)] = packed[None]

    def g_copy(o):
        return pltpu.make_async_remote_copy(
            src_ref=gram,
            dst_ref=grams.at[me],
            send_sem=g_send.at[o - 1],
            recv_sem=g_recv.at[o - 1],
            device_id={"dev": (me + o) % members},
            device_id_type=MESH,
        )

    def r_copy(o):
        return pltpu.make_async_remote_copy(
            src_ref=group_gram,
            dst_ref=group_grams.at[my_group],
            send_sem=r_send.at[o - 1],
            recv_sem=r_recv.at[o - 1],
            device_id={"grp": (my_group + o) % groups},
            device_id_type=MESH,
        )

    for o in range(1, members):
        g_copy(o).start()
    for o in range(1, members):
        g_copy(o).wait_recv()
    packed_group = functools.reduce(jnp.add, [grams[i] for i in range(members)])
    group_gram[...] = packed_group
    group_grams[pl.ds(my_group, 1)] = packed_group[None]
    for o in range(1, groups):
        r_copy(o).start()
    for o in range(1, groups):
        r_copy(o).wait_recv()
    sums_out[0] = packed_group
    sums_out[1] = functools.reduce(jnp.add, [group_grams[i] for i in range(groups)])

    for q in range(chunks):
        for xo in range(1, xs):
            for k in range(zs):
                x_copy(xo, q, k).wait_send()
        for k in range(1, team):
            mate_copy(k, q).wait_send()
        for k in range(team, zs):
            def sent(copy, k=k, q=q):
                copy(k, q).wait_send()

            if team > 1:
                pl.when(hands_over(k))(functools.partial(sent, mate_copy))
                pl.when(jnp.logical_not(hands_over(k)))(functools.partial(sent, far_copy))
            else:
                sent(far_copy)
    for o in range(1, members):
        g_copy(o).wait_send()
    for o in range(1, groups):
        r_copy(o).wait_send()
    save.wait()


def finish(members, groups, sample_hbm, leaf_gram, sums, basis, t_leaf, t_group, sample, load_sem):
    local, rank, leaf_rows = basis.shape
    load = pltpu.make_async_copy(sample_hbm, sample, load_sem)
    load.start()
    whole = leaf_gram[...]
    squares = [diagonal_block(whole, c, rank) for c in range(local)]
    factors = factor(squares + [unpack(sums[0], rank), unpack(sums[1], rank)])
    leaves, (group_upper, group_inverse), (_, root_inverse) = factors[:local], *factors[local:]
    for c in range(local):
        t_leaf[c] = dot(leaves[c][0], group_inverse, NT, HIGHEST) * math.sqrt(members * local)
    t_group[0] = dot(group_upper, root_inverse, NT, HIGHEST) * math.sqrt(groups)
    load.wait()
    for c in range(local):
        basis[c] = dot(
            leaves[c][1] * math.sqrt(leaf_rows), sample[c * rank : (c + 1) * rank], NN, HIGHEST
        )


def body(u_blocks, v_blocks, sketch, near_diag, block_row, col_count):
    blocks, rank, leaf_rows = u_blocks.shape
    local = sketch.shape[0]
    members = lax.axis_size("dev")
    groups = lax.axis_size("grp")
    xs = max(d for d in range(1, members + 1) if members % d == 0 and d * d <= members)
    zs = members // xs
    team = 2 if zs % 2 == 0 else 1
    chunks = leaf_rows // WIDTH
    slots = blocks * rank
    own = local * rank
    vmem = pl.BlockSpec(memory_space=pltpu.VMEM)
    smem = pl.BlockSpec(memory_space=pltpu.SMEM)
    hbm = pl.BlockSpec(memory_space=pl.ANY)
    dma = pltpu.SemaphoreType.DMA
    sample, leaf_gram, sums = pl.pallas_call(
        functools.partial(kernel, xs, local),
        out_shape=(
            jax.ShapeDtypeStruct((own, leaf_rows), F32),
            jax.ShapeDtypeStruct((own, own), F32),
            jax.ShapeDtypeStruct((2, 8, rank * rank // 8), F32),
        ),
        in_specs=[hbm, hbm, hbm, hbm, smem, smem],
        out_specs=(hbm, vmem, vmem),
        scratch_shapes=[
            pltpu.VMEM((own, leaf_rows), F32),
            pltpu.VMEM((local, leaf_rows), F32),
            pltpu.VMEM((slots, leaf_rows), F32),
            pltpu.VMEM((slots, leaf_rows), F32),
            pltpu.VMEM((slots, leaf_rows), BF16),
            pltpu.VMEM((slots, leaf_rows), BF16),
            pltpu.VMEM((xs, zs * own, slots), BF16),
            pltpu.VMEM((xs, zs * own, slots), BF16),
            pltpu.VMEM((xs, chunks, zs * own, WIDTH), F32),
            pltpu.VMEM((max(xs - 1, 1), chunks, zs * own, WIDTH), F32),
            pltpu.VMEM((max(zs - 1, 1), chunks, own, WIDTH), F32),
            pltpu.VMEM((max(zs // team - 1, 1), chunks, own, WIDTH), F32),
            pltpu.VMEM((own, leaf_rows), F32),
            pltpu.VMEM((8, rank * rank // 8), F32),
            pltpu.VMEM((members, 8, rank * rank // 8), F32),
            pltpu.VMEM((8, rank * rank // 8), F32),
            pltpu.VMEM((groups, 8, rank * rank // 8), F32),
            dma((2 + V_PARTS + chunks // PAIR,)),
            dma((max(xs - 1, 1), chunks, zs)),
            dma((max(xs - 1, 1), chunks, zs)),
            dma((max(zs - 1, 1), chunks)),
            dma((max(zs - 1, 1), chunks)),
            dma((max(zs - team, 1), chunks)),
            dma((max(zs // team - 1, 1), chunks)),
            dma((members - 1,)),
            dma((members - 1,)),
            dma((groups - 1,)),
            dma((groups - 1,)),
            pltpu.SemaphoreType.REGULAR((max(zs - 1, 1),)),
        ],
        compiler_params=pltpu.CompilerParams(
            collective_id=0, has_side_effects=True, vmem_limit_bytes=60 * 1024 * 1024
        ),
    )(
        u_blocks.reshape(slots, leaf_rows),
        v_blocks.reshape(slots, leaf_rows),
        sketch.reshape(own, leaf_rows),
        near_diag,
        block_row,
        col_count,
    )
    return pl.pallas_call(
        functools.partial(finish, members, groups),
        out_shape=(
            jax.ShapeDtypeStruct((local, rank, leaf_rows), F32),
            jax.ShapeDtypeStruct((local, rank, rank), F32),
            jax.ShapeDtypeStruct((1, rank, rank), F32),
        ),
        in_specs=[hbm, vmem, vmem],
        out_specs=(vmem, vmem, vmem),
        scratch_shapes=[pltpu.VMEM((own, leaf_rows), F32), dma],
    )(sample, leaf_gram, sums)


def solution(mesh):
    in_specs = (
        P(("grp", "dev"), None, None),
        P(("grp", "dev"), None, None),
        P(("grp", "dev"), None, None),
        P(("grp", "dev"), None),
        P(("grp", "dev")),
        P(("grp", "dev")),
    )
    out_specs = (P(("grp", "dev"), None, None), P(("grp", "dev"), None, None), P("grp", None, None))
    return jax.shard_map(body, mesh=mesh, in_specs=in_specs, out_specs=out_specs, check_vma=False)
```

```python
import functools
import math

import jax
import jax.numpy as jnp
from jax import lax
from jax.experimental import pallas as pl
from jax.experimental.pallas import tpu as pltpu
from jax.sharding import PartitionSpec as P

F32 = jnp.float32
BF16 = jnp.bfloat16
MESH = pl.DeviceIdType.MESH
HIGHEST = lax.Precision.HIGHEST
NN = (((1,), (0,)), ((), ()))
NT = (((1,), (1,)), ((), ()))
WIDTH = 128
PAIR = 2
V_PARTS = 3
PIVOTS = 8


def dot(a, b, dims, precision=None):
    return lax.dot_general(a, b, dims, precision=precision, preferred_element_type=F32)


def split(x):
    high = x.astype(BF16)
    return high, (x - high.astype(F32)).astype(BF16)


def dot3(a, b, dims):
    (ah, al), (bh, bl) = a, b
    return dot(ah, bh, dims) + dot(ah, bl, dims) + dot(al, bh, dims)


def pack(square):
    rank = square.shape[0]
    return jnp.concatenate([square[i : i + 8] for i in range(0, rank, 8)], axis=1)


def unpack(packed, rank):
    return jnp.concatenate([packed[:, i * rank : (i + 1) * rank] for i in range(rank // 8)], axis=0)


def diagonal_block(square, c, rank):
    at = slice(c * rank, (c + 1) * rank)
    return square[at, at]


def factor(grams):
    rank = grams[0].shape[0]
    rows = lax.broadcasted_iota(jnp.int32, (rank, 2 * rank), 0)
    lanes = lax.broadcasted_iota(jnp.int32, (rank, 2 * rank), 1)
    eye = (
        lax.broadcasted_iota(jnp.int32, (rank, rank), 0)
        == lax.broadcasted_iota(jnp.int32, (rank, rank), 1)
    ).astype(F32)
    state = [jnp.concatenate([g, eye], axis=1) for g in grams]
    for j in range(0, rank, PIVOTS):
        ahead = [
            [jnp.broadcast_to(m[:, j + b : j + b + 1], m.shape) for b in range(PIVOTS)] for m in state
        ]
        for b in range(min(PIVOTS, rank - 1 - j)):
            below = rows > j + b
            for n, m in enumerate(state):
                column = ahead[n][b]
                inverse = 1.0 / column[j + b : j + b + 1]
                low = jnp.where(below, column, 0.0)
                state[n] = m - low * (m[j + b : j + b + 1] * inverse)
                for e in range(b + 1, PIVOTS):
                    ahead[n][e] = ahead[n][e] - low * (column[j + e : j + e + 1] * inverse)
    out = []
    for m in state:
        diagonal = jnp.sum(jnp.where(rows == lanes, m, 0.0), axis=1, keepdims=True)
        m = m * lax.rsqrt(diagonal)
        upper = jnp.where((rows <= lanes)[:, :rank], m[:, :rank], 0.0)
        out.append((upper, m[:, rank:]))
    return out


def pieces_of(chunks):
    starts = list(range(0, chunks, PAIR))
    return [range(a, b) for a, b in zip(starts, starts[1:] + [chunks])]


def columns(piece):
    return pl.ds(piece.start * WIDTH, len(piece) * WIDTH)


def kernel(
    xs, local, u_hbm, v_hbm, sketch_hbm, diag_hbm, row_hbm, count_hbm, sample_out, squares_out,
    block_row, col_count, sketch, diag, u_buf, v_buf, u_high, u_low, w_high, w_low, part, got_x, got_mate, got_far, sample,
    gram, grams, group_gram, group_grams, uppers,
    load_sems, x_send, x_recv, m_send, m_recv, f_send, f_recv, g_send, g_recv, r_send, r_recv, relay,
):
    slots, leaf_rows = u_buf.shape
    rank = sample.shape[0] // local
    blocks = slots // rank
    members = grams.shape[0]
    groups = group_grams.shape[0]
    zs = members // xs
    chunks = leaf_rows // WIDTH
    own_rows = local * rank
    me = lax.axis_index("dev")
    my_group = lax.axis_index("grp")
    z, x = me // xs, me % xs

    pieces = pieces_of(chunks)
    near_loads = [
        pltpu.make_async_copy(sketch_hbm, sketch, load_sems.at[0]),
        pltpu.make_async_copy(diag_hbm, diag, load_sems.at[1]),
    ]
    v_rows = slots // V_PARTS
    v_loads = [
        pltpu.make_async_copy(
            v_hbm.at[pl.ds(i * v_rows, v_rows)],
            v_buf.at[pl.ds(i * v_rows, v_rows)],
            load_sems.at[2 + i],
        )
        for i in range(V_PARTS)
    ]
    u_loads = []
    for p, piece in enumerate(pieces):
        at = columns(piece)
        u_loads.append(
            pltpu.make_async_copy(
                u_hbm.at[:, at], u_buf.at[:, at], load_sems.at[4 + V_PARTS + p]
            )
        )
    index_loads = [
        pltpu.make_async_copy(row_hbm, block_row, load_sems.at[2 + V_PARTS]),
        pltpu.make_async_copy(count_hbm, col_count, load_sems.at[3 + V_PARTS]),
    ]
    for load in index_loads + near_loads[:1] + v_loads + u_loads + near_loads[1:]:
        load.start()
    barrier = pltpu.get_barrier_semaphore()
    for xo in range(1, xs):
        partner = z * xs + (x + xo) % xs
        pl.semaphore_signal(barrier, inc=1, device_id={"dev": partner}, device_id_type=MESH)
    for o in range(1, groups):
        pl.semaphore_signal(
            barrier, inc=1, device_id={"grp": (my_group + o) % groups}, device_id_type=MESH
        )

    def greet(semaphore):
        @pl.when(z > 0)
        def _():
            pl.semaphore_signal(
                semaphore, inc=1, device_id={"dev": me - xs}, device_id_type=MESH
            )

        @pl.when(z < zs - 1)
        def _():
            pl.semaphore_signal(
                semaphore, inc=1, device_id={"dev": me + xs}, device_id_type=MESH
            )

    team = 2 if zs % 2 == 0 else 1
    first, seat = z // team * team, z % team
    teams = zs // team

    def peer_z(k):
        if k == 0:
            return z
        if k < team:
            return first + (seat + k) % team
        return (first + k) % zs

    order = list(range(team, zs)) + list(range(1, team))
    near_z = jnp.where(z > 0, 1, 0) + jnp.where(z < zs - 1, 1, 0)
    greet(barrier)

    for load in index_loads:
        load.wait()
    lane = lax.broadcasted_iota(jnp.int32, (1, slots), 1)
    row_of = jnp.zeros((1, slots), jnp.int32)
    slot_of = jnp.zeros((1, slots), jnp.int32)
    for s in range(blocks):
        row_of = jnp.where(lane >= s * rank, block_row[s], row_of)
        slot_of = jnp.where(lane >= s * rank, s, slot_of)
    col_of = jnp.zeros((1, slots), jnp.int32)
    end = 0
    for c in range(local):
        end = end + col_count[c]
        col_of = col_of + jnp.where(slot_of >= end, 1, 0)

    near_loads[0].wait()
    sketch_parts = split(sketch[...])
    parts = []
    for i in range(V_PARTS):
        v_loads[i].wait()
        parts.append(dot3(sketch_parts, split(v_buf[i * v_rows : (i + 1) * v_rows]), NT))
    every = jnp.concatenate(parts, axis=1)
    coupling = jnp.zeros((rank, slots), F32)
    for c in range(local):
        coupling = coupling + jnp.where(col_of == c, every[c * rank : (c + 1) * rank], 0.0)
    high, low = (part_.astype(F32) for part_ in split(coupling))

    def place(xo):
        for zo in range(zs):
            dest = peer_z(zo) * xs + (x + xo) % xs
            for c in range(local):
                hit = row_of == dest * local + c
                at = pl.ds((zo * local + c) * rank, rank)
                w_high[xo, at, :] = jnp.where(hit, high, 0.0).astype(BF16)
                w_low[xo, at, :] = jnp.where(hit, low, 0.0).astype(BF16)

    for xo in range(1, xs):
        place(xo)

    def contribute(xo, piece):
        at = columns(piece)
        out = dot3((w_high[xo], w_low[xo]), (u_high[:, at], u_low[:, at]), NN)
        for h, q in enumerate(piece):
            part[xo, q] = out[:, h * WIDTH : (h + 1) * WIDTH]

    def x_copy(xo, q, k):
        at = pl.ds(k * own_rows, own_rows)
        return pltpu.make_async_remote_copy(
            src_ref=part.at[xo, q, at],
            dst_ref=got_x.at[xo - 1, q, at],
            send_sem=x_send.at[xo - 1, q, k],
            recv_sem=x_recv.at[xo - 1, q, k],
            device_id={"dev": z * xs + (x + xo) % xs},
            device_id_type=MESH,
        )

    def block(k):
        return pl.ds(k * own_rows, own_rows)

    def mate_copy(k, q):
        return pltpu.make_async_remote_copy(
            src_ref=part.at[0, q, block(k)],
            dst_ref=got_mate.at[k - 1, q],
            send_sem=m_send.at[k - 1, q],
            recv_sem=m_recv.at[k - 1, q],
            device_id={"dev": (first + team - 1 - seat) * xs + x},
            device_id_type=MESH,
        )

    def far_copy(k, q):
        slot = teams - k // team - 1
        return pltpu.make_async_remote_copy(
            src_ref=part.at[0, q, block(k)],
            dst_ref=got_far.at[slot, q],
            send_sem=f_send.at[k - team, q],
            recv_sem=f_recv.at[slot, q],
            device_id={"dev": peer_z(k) * xs + x},
            device_id_type=MESH,
        )

    def hands_over(k):
        return jnp.where(first + k < zs, 0, 1) == seat

    def pass_on(hop):
        pl.semaphore_wait(relay.at[hop], near_z)
        if hop < zs - 2:
            greet(relay.at[hop + 1])

    for p, piece in enumerate(pieces):
        at = columns(piece)
        u_loads[p].wait()
        u_high[:, at], u_low[:, at] = split(u_buf[:, at])
        for xo in range(1, xs):
            contribute(xo, piece)
        if p == 0:
            pl.semaphore_wait(barrier, xs - 1 + groups - 1 + near_z)
            greet(relay.at[0])
        for q in piece:
            for k in order:
                for xo in range(1, xs):
                    x_copy(xo, q, k).start()
    for q in range(chunks):
        for xo in range(1, xs):
            x_copy(xo, q, 0).start()
    for hop in range(zs - 1):
        pass_on(hop)
    place(0)

    def gather(k, q):
        total = part[0, q, block(k)]
        for xo in range(1, xs):
            x_copy(xo, q, k).wait_recv()
            total = total + got_x[xo - 1, q, block(k)]
        return total

    for piece in pieces:
        contribute(0, piece)
        for q in piece:
            for k in order:
                part[0, q, block(k)] = gather(k, q)
                if k < team:
                    mate_copy(k, q).start()
                elif team > 1:
                    @pl.when(hands_over(k))
                    def _(k=k, q=q):
                        mate_copy(k, q).start()
            for k in range(team, zs):
                def send_far(k=k, q=q):
                    if team > 1:
                        mate_copy(k, q).wait_recv()
                        part[0, q, block(k)] = part[0, q, block(k)] + got_mate[k - 1, q]
                    far_copy(k, q).start()

                if team > 1:
                    pl.when(jnp.logical_not(hands_over(k)))(send_far)
                else:
                    send_far()
    near_loads[1].wait()
    leaf_gram = jnp.zeros((own_rows, own_rows), F32)
    for q in range(chunks):
        at = pl.ds(q * WIDTH, WIDTH)
        near = [
            diag[c : c + 1, at] * sketch[c * rank : (c + 1) * rank, at] for c in range(local)
        ]
        total = gather(0, q) + jnp.concatenate(near, axis=0)
        for k in range(1, team):
            mate_copy(k, q).wait_recv()
            total = total + got_mate[k - 1, q]
        for k in range(team, zs, team):
            slot = teams - k // team - 1
            far_copy(k, q).wait_recv()
            total = total + got_far[slot, q]
        sample[:, at] = total
        leaf_gram = leaf_gram + dot(total, total, NT, HIGHEST)

    save = pltpu.make_async_copy(sample, sample_out, load_sems.at[0])
    save.start()
    squares = [diagonal_block(leaf_gram, c, rank) for c in range(local)]
    packed = pack(functools.reduce(jnp.add, squares))
    gram[...] = packed
    grams[pl.ds(me, 1)] = packed[None]

    def g_copy(o):
        return pltpu.make_async_remote_copy(
            src_ref=gram,
            dst_ref=grams.at[me],
            send_sem=g_send.at[o - 1],
            recv_sem=g_recv.at[o - 1],
            device_id={"dev": (me + o) % members},
            device_id_type=MESH,
        )

    def r_copy(o):
        return pltpu.make_async_remote_copy(
            src_ref=group_gram,
            dst_ref=group_grams.at[my_group],
            send_sem=r_send.at[o - 1],
            recv_sem=r_recv.at[o - 1],
            device_id={"grp": (my_group + o) % groups},
            device_id_type=MESH,
        )

    for o in range(1, members):
        g_copy(o).start()

    @pl.when(me < members)
    def _():
        for c, (upper, inverse) in enumerate(factor(squares)):
            uppers[c] = upper
            squares_out[local + c] = inverse * math.sqrt(leaf_rows)

    for o in range(1, members):
        g_copy(o).wait_recv()
    packed_group = functools.reduce(jnp.add, [grams[i] for i in range(members)])
    group_gram[...] = packed_group
    group_grams[pl.ds(my_group, 1)] = packed_group[None]
    for o in range(1, groups):
        r_copy(o).start()

    @pl.when(my_group < groups)
    def _():
        ((upper, inverse),) = factor([unpack(packed_group, rank)])
        for c in range(local):
            squares_out[c] = dot(uppers[c], inverse, NT, HIGHEST) * math.sqrt(members * local)
        squares_out[2 * local] = upper * math.sqrt(groups)

    for o in range(1, groups):
        r_copy(o).wait_recv()
    packed_root = functools.reduce(jnp.add, [group_grams[i] for i in range(groups)])
    squares_out[2 * local + 1] = unpack(packed_root, rank)

    for q in range(chunks):
        for xo in range(1, xs):
            for k in range(zs):
                x_copy(xo, q, k).wait_send()
        for k in range(1, team):
            mate_copy(k, q).wait_send()
        for k in range(team, zs):
            def sent(copy, k=k, q=q):
                copy(k, q).wait_send()

            if team > 1:
                pl.when(hands_over(k))(functools.partial(sent, mate_copy))
                pl.when(jnp.logical_not(hands_over(k)))(functools.partial(sent, far_copy))
            else:
                sent(far_copy)
    for o in range(1, members):
        g_copy(o).wait_send()
    for o in range(1, groups):
        r_copy(o).wait_send()
    save.wait()


def finish(sample_hbm, squares, basis, t_leaf, t_group, sample, load_sem):
    local, rank, _ = basis.shape
    load = pltpu.make_async_copy(sample_hbm, sample, load_sem)
    load.start()
    for c in range(local):
        t_leaf[c] = squares[c]
    ((_, root_inverse),) = factor([squares[2 * local + 1]])
    t_group[0] = dot(squares[2 * local], root_inverse, NT, HIGHEST)
    load.wait()
    for c in range(local):
        basis[c] = dot(squares[local + c], sample[c * rank : (c + 1) * rank], NN, HIGHEST)


def body(u_blocks, v_blocks, sketch, near_diag, block_row, col_count):
    blocks, rank, leaf_rows = u_blocks.shape
    local = sketch.shape[0]
    members = lax.axis_size("dev")
    groups = lax.axis_size("grp")
    xs = max(d for d in range(1, members + 1) if members % d == 0 and d * d <= members)
    zs = members // xs
    team = 2 if zs % 2 == 0 else 1
    chunks = leaf_rows // WIDTH
    slots = blocks * rank
    own = local * rank
    vmem = pl.BlockSpec(memory_space=pltpu.VMEM)
    hbm = pl.BlockSpec(memory_space=pl.ANY)
    dma = pltpu.SemaphoreType.DMA
    sample, squares = pl.pallas_call(
        functools.partial(kernel, xs, local),
        out_shape=(
            jax.ShapeDtypeStruct((own, leaf_rows), F32),
            jax.ShapeDtypeStruct((2 * local + 2, rank, rank), F32),
        ),
        in_specs=[hbm] * 6,
        out_specs=(hbm, vmem),
        scratch_shapes=[
            pltpu.SMEM((blocks,), jnp.int32),
            pltpu.SMEM((local,), jnp.int32),
            pltpu.VMEM((own, leaf_rows), F32),
            pltpu.VMEM((local, leaf_rows), F32),
            pltpu.VMEM((slots, leaf_rows), F32),
            pltpu.VMEM((slots, leaf_rows), F32),
            pltpu.VMEM((slots, leaf_rows), BF16),
            pltpu.VMEM((slots, leaf_rows), BF16),
            pltpu.VMEM((xs, zs * own, slots), BF16),
            pltpu.VMEM((xs, zs * own, slots), BF16),
            pltpu.VMEM((xs, chunks, zs * own, WIDTH), F32),
            pltpu.VMEM((max(xs - 1, 1), chunks, zs * own, WIDTH), F32),
            pltpu.VMEM((max(zs - 1, 1), chunks, own, WIDTH), F32),
            pltpu.VMEM((max(zs // team - 1, 1), chunks, own, WIDTH), F32),
            pltpu.VMEM((own, leaf_rows), F32),
            pltpu.VMEM((8, rank * rank // 8), F32),
            pltpu.VMEM((members, 8, rank * rank // 8), F32),
            pltpu.VMEM((8, rank * rank // 8), F32),
            pltpu.VMEM((groups, 8, rank * rank // 8), F32),
            pltpu.VMEM((local, rank, rank), F32),
            dma((4 + V_PARTS + len(pieces_of(chunks)),)),
            dma((max(xs - 1, 1), chunks, zs)),
            dma((max(xs - 1, 1), chunks, zs)),
            dma((max(zs - 1, 1), chunks)),
            dma((max(zs - 1, 1), chunks)),
            dma((max(zs - team, 1), chunks)),
            dma((max(zs // team - 1, 1), chunks)),
            dma((members - 1,)),
            dma((members - 1,)),
            dma((groups - 1,)),
            dma((groups - 1,)),
            pltpu.SemaphoreType.REGULAR((max(zs - 1, 1),)),
        ],
        compiler_params=pltpu.CompilerParams(
            collective_id=0, has_side_effects=True, vmem_limit_bytes=60 * 1024 * 1024
        ),
    )(
        u_blocks.reshape(slots, leaf_rows),
        v_blocks.reshape(slots, leaf_rows),
        sketch.reshape(own, leaf_rows),
        near_diag,
        block_row,
        col_count,
    )
    return pl.pallas_call(
        finish,
        out_shape=(
            jax.ShapeDtypeStruct((local, rank, leaf_rows), F32),
            jax.ShapeDtypeStruct((local, rank, rank), F32),
            jax.ShapeDtypeStruct((1, rank, rank), F32),
        ),
        in_specs=[hbm, vmem],
        out_specs=(vmem, vmem, vmem),
        scratch_shapes=[pltpu.VMEM((own, leaf_rows), F32), dma],
    )(sample, squares)


def solution(mesh):
    in_specs = (
        P(("grp", "dev"), None, None),
        P(("grp", "dev"), None, None),
        P(("grp", "dev"), None, None),
        P(("grp", "dev"), None),
        P(("grp", "dev")),
        P(("grp", "dev")),
    )
    out_specs = (P(("grp", "dev"), None, None), P(("grp", "dev"), None, None), P("grp", None, None))
    return jax.shard_map(body, mesh=mesh, in_specs=in_specs, out_specs=out_specs, check_vma=False)
```

```python
import functools
import math

import jax
import jax.numpy as jnp
from jax import lax
from jax.experimental import pallas as pl
from jax.experimental.pallas import tpu as pltpu
from jax.sharding import PartitionSpec as P

F32 = jnp.float32
BF16 = jnp.bfloat16
MESH = pl.DeviceIdType.MESH
HIGHEST = lax.Precision.HIGHEST
NN = (((1,), (0,)), ((), ()))
NT = (((1,), (1,)), ((), ()))
WIDTH = 128
PAIR = 2
V_PARTS = 3
PIVOTS = 8


def dot(a, b, dims, precision=None):
    return lax.dot_general(a, b, dims, precision=precision, preferred_element_type=F32)


def split(x):
    high = x.astype(BF16)
    return high, (x - high.astype(F32)).astype(BF16)


def dot3(a, b, dims):
    (ah, al), (bh, bl) = a, b
    return dot(ah, bh, dims) + dot(ah, bl, dims) + dot(al, bh, dims)


def pack(square):
    rank = square.shape[0]
    return jnp.concatenate([square[i : i + 8] for i in range(0, rank, 8)], axis=1)


def unpack(packed, rank):
    return jnp.concatenate([packed[:, i * rank : (i + 1) * rank] for i in range(rank // 8)], axis=0)


def diagonal_block(square, c, rank):
    at = slice(c * rank, (c + 1) * rank)
    return square[at, at]


def factor(grams):
    rank = grams[0].shape[0]
    rows = lax.broadcasted_iota(jnp.int32, (rank, 2 * rank), 0)
    lanes = lax.broadcasted_iota(jnp.int32, (rank, 2 * rank), 1)
    eye = (
        lax.broadcasted_iota(jnp.int32, (rank, rank), 0)
        == lax.broadcasted_iota(jnp.int32, (rank, rank), 1)
    ).astype(F32)
    state = [jnp.concatenate([g, eye], axis=1) for g in grams]
    for j in range(0, rank, PIVOTS):
        ahead = [
            [jnp.broadcast_to(m[:, j + b : j + b + 1], m.shape) for b in range(PIVOTS)] for m in state
        ]
        for b in range(min(PIVOTS, rank - 1 - j)):
            below = rows > j + b
            for n, m in enumerate(state):
                column = ahead[n][b]
                inverse = 1.0 / column[j + b : j + b + 1]
                low = jnp.where(below, column, 0.0)
                state[n] = m - low * (m[j + b : j + b + 1] * inverse)
                for e in range(b + 1, PIVOTS):
                    ahead[n][e] = ahead[n][e] - low * (column[j + e : j + e + 1] * inverse)
    out = []
    for m in state:
        diagonal = jnp.sum(jnp.where(rows == lanes, m, 0.0), axis=1, keepdims=True)
        m = m * lax.rsqrt(diagonal)
        upper = jnp.where((rows <= lanes)[:, :rank], m[:, :rank], 0.0)
        out.append((upper, m[:, rank:]))
    return out


def pieces_of(chunks, early):
    starts = list(range(early, chunks, PAIR))
    return [range(a, b) for a, b in zip(starts, starts[1:] + [chunks])]


def early_of(chunks, xs, zs):
    return chunks // 8 if xs > 1 and zs > 2 and zs % 2 == 0 else 0


def columns(piece):
    return pl.ds(piece.start * WIDTH, len(piece) * WIDTH)


def kernel(
    xs, local, u_hbm, v_hbm, sketch_hbm, diag_hbm, row_hbm, count_hbm, sample_out, squares_out,
    block_row, col_count, sketch, diag, u_buf, v_buf, u_high, u_low, w_high, w_low, part, got_x, got_mate, got_far, sample,
    gram, grams, group_gram, group_grams, uppers,
    load_sems, x_send, x_recv, m_send, m_recv, f_send, f_recv, g_send, g_recv, r_send, r_recv, relay,
):
    slots, leaf_rows = u_buf.shape
    rank = sample.shape[0] // local
    blocks = slots // rank
    members = grams.shape[0]
    groups = group_grams.shape[0]
    zs = members // xs
    chunks = leaf_rows // WIDTH
    own_rows = local * rank
    me = lax.axis_index("dev")
    my_group = lax.axis_index("grp")
    z, x = me // xs, me % xs

    early = early_of(chunks, xs, zs)
    pieces = pieces_of(chunks, early)
    loads = pieces + ([range(early)] if early else [])
    loads = loads[:1] + loads[len(pieces) :] + loads[1 : len(pieces)]
    near_loads = [
        pltpu.make_async_copy(sketch_hbm, sketch, load_sems.at[0]),
        pltpu.make_async_copy(diag_hbm, diag, load_sems.at[1]),
    ]
    v_rows = slots // V_PARTS
    v_loads = [
        pltpu.make_async_copy(
            v_hbm.at[pl.ds(i * v_rows, v_rows)],
            v_buf.at[pl.ds(i * v_rows, v_rows)],
            load_sems.at[2 + i],
        )
        for i in range(V_PARTS)
    ]
    u_loads = []
    for p, piece in enumerate(loads):
        at = columns(piece)
        u_loads.append(
            pltpu.make_async_copy(
                u_hbm.at[:, at], u_buf.at[:, at], load_sems.at[4 + V_PARTS + p]
            )
        )
    index_loads = [
        pltpu.make_async_copy(row_hbm, block_row, load_sems.at[2 + V_PARTS]),
        pltpu.make_async_copy(count_hbm, col_count, load_sems.at[3 + V_PARTS]),
    ]
    for load in index_loads + near_loads[:1] + v_loads + u_loads + near_loads[1:]:
        load.start()
    barrier = pltpu.get_barrier_semaphore()
    for xo in range(1, xs):
        partner = z * xs + (x + xo) % xs
        pl.semaphore_signal(barrier, inc=1, device_id={"dev": partner}, device_id_type=MESH)
    for o in range(1, groups):
        pl.semaphore_signal(
            barrier, inc=1, device_id={"grp": (my_group + o) % groups}, device_id_type=MESH
        )

    def greet(semaphore):
        @pl.when(z > 0)
        def _():
            pl.semaphore_signal(
                semaphore, inc=1, device_id={"dev": me - xs}, device_id_type=MESH
            )

        @pl.when(z < zs - 1)
        def _():
            pl.semaphore_signal(
                semaphore, inc=1, device_id={"dev": me + xs}, device_id_type=MESH
            )

    team = 2 if zs % 2 == 0 else 1
    first, seat = z // team * team, z % team
    teams = zs // team

    def peer_z(k):
        if k == 0:
            return z
        if k < team:
            return first + (seat + k) % team
        return (first + k) % zs

    order = list(range(team, zs)) + list(range(1, team))
    near_z = jnp.where(z > 0, 1, 0) + jnp.where(z < zs - 1, 1, 0)
    greet(barrier)

    for load in index_loads:
        load.wait()
    lane = lax.broadcasted_iota(jnp.int32, (1, slots), 1)
    row_of = jnp.zeros((1, slots), jnp.int32)
    slot_of = jnp.zeros((1, slots), jnp.int32)
    for s in range(blocks):
        row_of = jnp.where(lane >= s * rank, block_row[s], row_of)
        slot_of = jnp.where(lane >= s * rank, s, slot_of)
    col_of = jnp.zeros((1, slots), jnp.int32)
    end = 0
    for c in range(local):
        end = end + col_count[c]
        col_of = col_of + jnp.where(slot_of >= end, 1, 0)

    near_loads[0].wait()
    sketch_parts = split(sketch[...])
    parts = []
    for i in range(V_PARTS):
        v_loads[i].wait()
        parts.append(dot3(sketch_parts, split(v_buf[i * v_rows : (i + 1) * v_rows]), NT))
    every = jnp.concatenate(parts, axis=1)
    coupling = jnp.zeros((rank, slots), F32)
    for c in range(local):
        coupling = coupling + jnp.where(col_of == c, every[c * rank : (c + 1) * rank], 0.0)
    high, low = (part_.astype(F32) for part_ in split(coupling))

    def place(xo):
        for zo in range(zs):
            dest = peer_z(zo) * xs + (x + xo) % xs
            for c in range(local):
                hit = row_of == dest * local + c
                at = pl.ds((zo * local + c) * rank, rank)
                w_high[xo, at, :] = jnp.where(hit, high, 0.0).astype(BF16)
                w_low[xo, at, :] = jnp.where(hit, low, 0.0).astype(BF16)

    for xo in range(1, xs):
        place(xo)

    def contribute(xo, piece):
        at = columns(piece)
        out = dot3((w_high[xo], w_low[xo]), (u_high[:, at], u_low[:, at]), NN)
        for h, q in enumerate(piece):
            part[xo, q] = out[:, h * WIDTH : (h + 1) * WIDTH]

    def x_copy(xo, q, k):
        at = pl.ds(k * own_rows, own_rows)
        return pltpu.make_async_remote_copy(
            src_ref=part.at[xo, q, at],
            dst_ref=got_x.at[xo - 1, q, at],
            send_sem=x_send.at[xo - 1, q, k],
            recv_sem=x_recv.at[xo - 1, q, k],
            device_id={"dev": z * xs + (x + xo) % xs},
            device_id_type=MESH,
        )

    def block(k):
        return pl.ds(k * own_rows, own_rows)

    def lane_of(q, xo):
        return q if xo == 0 else chunks + (xo - 1) * early + q

    def mate_copy(k, q, xo=0):
        return pltpu.make_async_remote_copy(
            src_ref=part.at[xo, q, block(k)],
            dst_ref=got_mate.at[k - 1, lane_of(q, xo)],
            send_sem=m_send.at[k - 1, lane_of(q, xo)],
            recv_sem=m_recv.at[k - 1, lane_of(q, xo)],
            device_id={"dev": (first + team - 1 - seat) * xs + x},
            device_id_type=MESH,
        )

    def far_copy(k, q, xo=0):
        slot = teams - k // team - 1
        return pltpu.make_async_remote_copy(
            src_ref=part.at[xo, q, block(k)],
            dst_ref=got_far.at[slot, lane_of(q, xo)],
            send_sem=f_send.at[k - team, lane_of(q, xo)],
            recv_sem=f_recv.at[slot, lane_of(q, xo)],
            device_id={"dev": peer_z(k) * xs + x},
            device_id_type=MESH,
        )

    def hands_over(k):
        return jnp.where(first + k < zs, 0, 1) == seat

    def pass_on(hop):
        pl.semaphore_wait(relay.at[hop], near_z)
        if hop < zs - 2:
            greet(relay.at[hop + 1])

    def gather(k, q):
        total = part[0, q, block(k)]
        for xo in range(1, xs):
            x_copy(xo, q, k).wait_recv()
            total = total + got_x[xo - 1, q, block(k)]
        return total

    def to_mate(k, q, xo):
        if k < team:
            mate_copy(k, q, xo).start()
        elif team > 1:
            @pl.when(hands_over(k))
            def _():
                mate_copy(k, q, xo).start()

    def to_far(k, q, xo):
        def send():
            if team > 1:
                mate_copy(k, q, xo).wait_recv()
                got = got_mate[k - 1, lane_of(q, xo)]
                part[xo, q, block(k)] = part[xo, q, block(k)] + got
            far_copy(k, q, xo).start()

        if team > 1:
            pl.when(jnp.logical_not(hands_over(k)))(send)
        else:
            send()

    def arrived(q, xo):
        got = []
        for k in range(1, team):
            mate_copy(k, q, xo).wait_recv()
            got.append(got_mate[k - 1, lane_of(q, xo)])
        for k in range(team, zs, team):
            far_copy(k, q, xo).wait_recv()
            got.append(got_far[teams - k // team - 1, lane_of(q, xo)])
        return functools.reduce(jnp.add, got)

    def along_z(piece):
        contribute(0, piece)
        for q in piece:
            for k in order:
                part[0, q, block(k)] = gather(k, q)
                to_mate(k, q, 0)
            for k in range(team, zs):
                to_far(k, q, 0)

    def load(piece):
        at = columns(piece)
        u_loads[loads.index(piece)].wait()
        u_high[:, at], u_low[:, at] = split(u_buf[:, at])

    for p, piece in enumerate(pieces):
        load(piece)
        for xo in range(1, xs):
            contribute(xo, piece)
        if p == 0:
            pl.semaphore_wait(barrier, xs - 1 + groups - 1 + near_z)
            greet(relay.at[0])
        for q in piece:
            for k in order:
                for xo in range(1, xs):
                    x_copy(xo, q, k).start()
        if p == 0:
            place(0)
            if early:
                load(range(early))
                for xo in range(xs):
                    contribute(xo, range(early))
                for q in range(early):
                    for k in order:
                        for xo in range(xs):
                            to_mate(k, q, xo)
        if p == 1:
            for hop in range(zs - 1):
                pass_on(hop)
            for q in range(early):
                for k in range(team, zs):
                    for xo in range(xs):
                        to_far(k, q, xo)
        if p == len(pieces) - 1:
            for q in range(early):
                for xo in range(1, xs):
                    part[xo, q, block(0)] = part[xo, q, block(0)] + arrived(q, xo)
            for q in range(chunks):
                for xo in range(1, xs):
                    x_copy(xo, q, 0).start()
        if p > 0:
            along_z(pieces[p - 1])
    along_z(pieces[-1])
    near_loads[1].wait()
    leaf_gram = jnp.zeros((own_rows, own_rows), F32)
    for q in range(chunks):
        at = pl.ds(q * WIDTH, WIDTH)
        near = [
            diag[c : c + 1, at] * sketch[c * rank : (c + 1) * rank, at] for c in range(local)
        ]
        total = gather(0, q) + jnp.concatenate(near, axis=0) + arrived(q, 0)
        sample[:, at] = total
        leaf_gram = leaf_gram + dot(total, total, NT, HIGHEST)

    save = pltpu.make_async_copy(sample, sample_out, load_sems.at[0])
    save.start()
    squares = [diagonal_block(leaf_gram, c, rank) for c in range(local)]
    packed = pack(functools.reduce(jnp.add, squares))
    gram[...] = packed
    grams[pl.ds(me, 1)] = packed[None]

    def g_copy(o):
        return pltpu.make_async_remote_copy(
            src_ref=gram,
            dst_ref=grams.at[me],
            send_sem=g_send.at[o - 1],
            recv_sem=g_recv.at[o - 1],
            device_id={"dev": (me + o) % members},
            device_id_type=MESH,
        )

    def r_copy(o):
        return pltpu.make_async_remote_copy(
            src_ref=group_gram,
            dst_ref=group_grams.at[my_group],
            send_sem=r_send.at[o - 1],
            recv_sem=r_recv.at[o - 1],
            device_id={"grp": (my_group + o) % groups},
            device_id_type=MESH,
        )

    for o in range(1, members):
        g_copy(o).start()

    @pl.when(me < members)
    def _():
        for c, (upper, inverse) in enumerate(factor(squares)):
            uppers[c] = upper
            squares_out[local + c] = inverse * math.sqrt(leaf_rows)

    for o in range(1, members):
        g_copy(o).wait_recv()
    packed_group = functools.reduce(jnp.add, [grams[i] for i in range(members)])
    group_gram[...] = packed_group
    group_grams[pl.ds(my_group, 1)] = packed_group[None]
    for o in range(1, groups):
        r_copy(o).start()

    @pl.when(my_group < groups)
    def _():
        ((upper, inverse),) = factor([unpack(packed_group, rank)])
        for c in range(local):
            squares_out[c] = dot(uppers[c], inverse, NT, HIGHEST) * math.sqrt(members * local)
        squares_out[2 * local] = upper * math.sqrt(groups)

    for o in range(1, groups):
        r_copy(o).wait_recv()
    packed_root = functools.reduce(jnp.add, [group_grams[i] for i in range(groups)])
    squares_out[2 * local + 1] = unpack(packed_root, rank)

    for q in range(chunks):
        for xo in range(1, xs):
            for k in range(1 if q < early else zs):
                x_copy(xo, q, k).wait_send()
        for xo in range(xs if q < early else 1):
            for k in range(1, team):
                mate_copy(k, q, xo).wait_send()
            for k in range(team, zs):
                def sent(copy, k=k, q=q, xo=xo):
                    copy(k, q, xo).wait_send()

                if team > 1:
                    pl.when(hands_over(k))(functools.partial(sent, mate_copy))
                    pl.when(jnp.logical_not(hands_over(k)))(functools.partial(sent, far_copy))
                else:
                    sent(far_copy)
    for o in range(1, members):
        g_copy(o).wait_send()
    for o in range(1, groups):
        r_copy(o).wait_send()
    save.wait()


def finish(sample_hbm, squares, basis, t_leaf, t_group, sample, load_sem):
    local, rank, _ = basis.shape
    load = pltpu.make_async_copy(sample_hbm, sample, load_sem)
    load.start()
    for c in range(local):
        t_leaf[c] = squares[c]
    ((_, root_inverse),) = factor([squares[2 * local + 1]])
    t_group[0] = dot(squares[2 * local], root_inverse, NT, HIGHEST)
    load.wait()
    for c in range(local):
        basis[c] = dot(squares[local + c], sample[c * rank : (c + 1) * rank], NN, HIGHEST)


def body(u_blocks, v_blocks, sketch, near_diag, block_row, col_count):
    blocks, rank, leaf_rows = u_blocks.shape
    local = sketch.shape[0]
    members = lax.axis_size("dev")
    groups = lax.axis_size("grp")
    xs = max(d for d in range(1, members + 1) if members % d == 0 and d * d <= members)
    zs = members // xs
    team = 2 if zs % 2 == 0 else 1
    chunks = leaf_rows // WIDTH
    early = early_of(chunks, xs, zs)
    lanes = chunks + (xs - 1) * early
    slots = blocks * rank
    own = local * rank
    vmem = pl.BlockSpec(memory_space=pltpu.VMEM)
    hbm = pl.BlockSpec(memory_space=pl.ANY)
    dma = pltpu.SemaphoreType.DMA
    sample, squares = pl.pallas_call(
        functools.partial(kernel, xs, local),
        out_shape=(
            jax.ShapeDtypeStruct((own, leaf_rows), F32),
            jax.ShapeDtypeStruct((2 * local + 2, rank, rank), F32),
        ),
        in_specs=[hbm] * 6,
        out_specs=(hbm, vmem),
        scratch_shapes=[
            pltpu.SMEM((blocks,), jnp.int32),
            pltpu.SMEM((local,), jnp.int32),
            pltpu.VMEM((own, leaf_rows), F32),
            pltpu.VMEM((local, leaf_rows), F32),
            pltpu.VMEM((slots, leaf_rows), F32),
            pltpu.VMEM((slots, leaf_rows), F32),
            pltpu.VMEM((slots, leaf_rows), BF16),
            pltpu.VMEM((slots, leaf_rows), BF16),
            pltpu.VMEM((xs, zs * own, slots), BF16),
            pltpu.VMEM((xs, zs * own, slots), BF16),
            pltpu.VMEM((xs, chunks, zs * own, WIDTH), F32),
            pltpu.VMEM((max(xs - 1, 1), chunks, zs * own, WIDTH), F32),
            pltpu.VMEM((max(zs - 1, 1), lanes, own, WIDTH), F32),
            pltpu.VMEM((max(zs // team - 1, 1), lanes, own, WIDTH), F32),
            pltpu.VMEM((own, leaf_rows), F32),
            pltpu.VMEM((8, rank * rank // 8), F32),
            pltpu.VMEM((members, 8, rank * rank // 8), F32),
            pltpu.VMEM((8, rank * rank // 8), F32),
            pltpu.VMEM((groups, 8, rank * rank // 8), F32),
            pltpu.VMEM((local, rank, rank), F32),
            dma((5 + V_PARTS + len(pieces_of(chunks, early)),)),
            dma((max(xs - 1, 1), chunks, zs)),
            dma((max(xs - 1, 1), chunks, zs)),
            dma((max(zs - 1, 1), lanes)),
            dma((max(zs - 1, 1), lanes)),
            dma((max(zs - team, 1), lanes)),
            dma((max(zs // team - 1, 1), lanes)),
            dma((members - 1,)),
            dma((members - 1,)),
            dma((groups - 1,)),
            dma((groups - 1,)),
            pltpu.SemaphoreType.REGULAR((max(zs - 1, 1),)),
        ],
        compiler_params=pltpu.CompilerParams(
            collective_id=0, has_side_effects=True, vmem_limit_bytes=60 * 1024 * 1024
        ),
    )(
        u_blocks.reshape(slots, leaf_rows),
        v_blocks.reshape(slots, leaf_rows),
        sketch.reshape(own, leaf_rows),
        near_diag,
        block_row,
        col_count,
    )
    return pl.pallas_call(
        finish,
        out_shape=(
            jax.ShapeDtypeStruct((local, rank, leaf_rows), F32),
            jax.ShapeDtypeStruct((local, rank, rank), F32),
            jax.ShapeDtypeStruct((1, rank, rank), F32),
        ),
        in_specs=[hbm, vmem],
        out_specs=(vmem, vmem, vmem),
        scratch_shapes=[pltpu.VMEM((own, leaf_rows), F32), dma],
    )(sample, squares)


def solution(mesh):
    in_specs = (
        P(("grp", "dev"), None, None),
        P(("grp", "dev"), None, None),
        P(("grp", "dev"), None, None),
        P(("grp", "dev"), None),
        P(("grp", "dev")),
        P(("grp", "dev")),
    )
    out_specs = (P(("grp", "dev"), None, None), P(("grp", "dev"), None, None), P("grp", None, None))
    return jax.shard_map(body, mesh=mesh, in_specs=in_specs, out_specs=out_specs, check_vma=False)
```

```python
import functools
import math

import jax
import jax.numpy as jnp
from jax import lax
from jax.experimental import pallas as pl
from jax.experimental.pallas import tpu as pltpu
from jax.sharding import PartitionSpec as P

F32 = jnp.float32
BF16 = jnp.bfloat16
MESH = pl.DeviceIdType.MESH
HIGHEST = lax.Precision.HIGHEST
NN = (((1,), (0,)), ((), ()))
NT = (((1,), (1,)), ((), ()))
WIDTH = 128
PAIR = 2
V_PARTS = 1
PIVOTS = 16


def dot(a, b, dims, precision=None):
    return lax.dot_general(a, b, dims, precision=precision, preferred_element_type=F32)


def split(x):
    high = x.astype(BF16)
    return high, (x - high.astype(F32)).astype(BF16)


def dot3(a, b, dims):
    (ah, al), (bh, bl) = a, b
    return dot(ah, bh, dims) + dot(ah, bl, dims) + dot(al, bh, dims)


def dot3_stacked(a, b, dims):
    (high, rest), (bh, bl) = a, b
    rows = high.shape[0]
    both = dot(jnp.concatenate([high, rest], axis=0), bh, dims)
    return both[:rows] + both[rows:] + dot(high, bl, dims)


def pack(square):
    rank = square.shape[0]
    return jnp.concatenate([square[i : i + 8] for i in range(0, rank, 8)], axis=1)


def unpack(packed, rank):
    return jnp.concatenate([packed[:, i * rank : (i + 1) * rank] for i in range(rank // 8)], axis=0)


def diagonal_block(square, c, rank):
    at = slice(c * rank, (c + 1) * rank)
    return square[at, at]


def factor(grams):
    rank = grams[0].shape[0]
    rows = lax.broadcasted_iota(jnp.int32, (rank, 2 * rank), 0)
    lanes = lax.broadcasted_iota(jnp.int32, (rank, 2 * rank), 1)
    eye = (
        lax.broadcasted_iota(jnp.int32, (rank, rank), 0)
        == lax.broadcasted_iota(jnp.int32, (rank, rank), 1)
    ).astype(F32)
    state = [jnp.concatenate([g, eye], axis=1) for g in grams]
    for j in range(0, rank, PIVOTS):
        ahead = [
            [jnp.broadcast_to(m[:, j + b : j + b + 1], m.shape) for b in range(PIVOTS)] for m in state
        ]
        for b in range(min(PIVOTS, rank - 1 - j)):
            below = rows > j + b
            for n, m in enumerate(state):
                column = ahead[n][b]
                inverse = 1.0 / column[j + b : j + b + 1]
                low = jnp.where(below, column, 0.0)
                state[n] = m - low * (m[j + b : j + b + 1] * inverse)
                for e in range(b + 1, PIVOTS):
                    ahead[n][e] = ahead[n][e] - low * (column[j + e : j + e + 1] * inverse)
    out = []
    for m in state:
        diagonal = jnp.sum(jnp.where(rows == lanes, m, 0.0), axis=1, keepdims=True)
        m = m * lax.rsqrt(diagonal)
        upper = jnp.where((rows <= lanes)[:, :rank], m[:, :rank], 0.0)
        out.append((upper, m[:, rank:]))
    return out


def pieces_of(chunks, early):
    starts = list(range(early, chunks, PAIR))
    return [range(a, b) for a, b in zip(starts, starts[1:] + [chunks])]


def early_of(chunks, xs, zs):
    return chunks // 8 if xs > 1 and zs > 2 and zs % 2 == 0 else 0


def columns(piece):
    return pl.ds(piece.start * WIDTH, len(piece) * WIDTH)


def kernel(
    xs, local, u_hbm, v_hbm, sketch_hbm, diag_hbm, row_hbm, count_hbm, sample_out, squares_out,
    block_row, col_count, sketch, diag, u_buf, v_buf, u_high, u_low, w_high, w_low, part, got_x, got_mate, got_far, sample,
    gram, grams, group_gram, group_grams, uppers,
    load_sems, x_send, x_recv, m_send, m_recv, f_send, f_recv, g_send, g_recv, r_send, r_recv, relay,
):
    slots, leaf_rows = u_buf.shape
    rank = sample.shape[0] // local
    blocks = slots // rank
    members = grams.shape[0]
    groups = group_grams.shape[0]
    zs = members // xs
    chunks = leaf_rows // WIDTH
    own_rows = local * rank
    me = lax.axis_index("dev")
    my_group = lax.axis_index("grp")
    z, x = me // xs, me % xs

    early = early_of(chunks, xs, zs)
    pieces = pieces_of(chunks, early)
    loads = pieces + ([range(early)] if early else [])
    loads = loads[:1] + loads[len(pieces) :] + loads[1 : len(pieces)]
    near_loads = [
        pltpu.make_async_copy(sketch_hbm, sketch, load_sems.at[0]),
        pltpu.make_async_copy(diag_hbm, diag, load_sems.at[1]),
    ]
    v_rows = slots // V_PARTS
    v_loads = [
        pltpu.make_async_copy(
            v_hbm.at[pl.ds(i * v_rows, v_rows)],
            v_buf.at[pl.ds(i * v_rows, v_rows)],
            load_sems.at[2 + i],
        )
        for i in range(V_PARTS)
    ]
    u_loads = []
    for p, piece in enumerate(loads):
        at = columns(piece)
        u_loads.append(
            pltpu.make_async_copy(
                u_hbm.at[:, at], u_buf.at[:, at], load_sems.at[4 + V_PARTS + p]
            )
        )
    index_loads = [
        pltpu.make_async_copy(row_hbm, block_row, load_sems.at[2 + V_PARTS]),
        pltpu.make_async_copy(count_hbm, col_count, load_sems.at[3 + V_PARTS]),
    ]
    for load in index_loads + near_loads[:1] + v_loads + u_loads[:1] + u_loads[1:] + near_loads[1:]:
        load.start()
    barrier = pltpu.get_barrier_semaphore()
    for xo in range(1, xs):
        partner = z * xs + (x + xo) % xs
        pl.semaphore_signal(barrier, inc=1, device_id={"dev": partner}, device_id_type=MESH)
    for o in range(1, groups):
        pl.semaphore_signal(
            barrier, inc=1, device_id={"grp": (my_group + o) % groups}, device_id_type=MESH
        )

    def greet(semaphore):
        @pl.when(z > 0)
        def _():
            pl.semaphore_signal(
                semaphore, inc=1, device_id={"dev": me - xs}, device_id_type=MESH
            )

        @pl.when(z < zs - 1)
        def _():
            pl.semaphore_signal(
                semaphore, inc=1, device_id={"dev": me + xs}, device_id_type=MESH
            )

    team = 2 if zs % 2 == 0 else 1
    first, seat = z // team * team, z % team
    teams = zs // team

    def peer_z(k):
        if k == 0:
            return z
        if k < team:
            return first + (seat + k) % team
        return (first + k) % zs

    order = list(range(team, zs)) + list(range(1, team))
    near_z = jnp.where(z > 0, 1, 0) + jnp.where(z < zs - 1, 1, 0)
    greet(barrier)

    for load in index_loads:
        load.wait()
    lane = lax.broadcasted_iota(jnp.int32, (1, slots), 1)
    row_of = jnp.zeros((1, slots), jnp.int32)
    slot_of = jnp.zeros((1, slots), jnp.int32)
    for s in range(blocks):
        row_of = jnp.where(lane >= s * rank, block_row[s], row_of)
        slot_of = jnp.where(lane >= s * rank, s, slot_of)
    col_of = jnp.zeros((1, slots), jnp.int32)
    end = 0
    for c in range(local):
        end = end + col_count[c]
        col_of = col_of + jnp.where(slot_of >= end, 1, 0)

    near_loads[0].wait()
    sketch_parts = split(sketch[...])
    parts = []
    for i in range(V_PARTS):
        v_loads[i].wait()
        parts.append(dot3_stacked(sketch_parts, split(v_buf[i * v_rows : (i + 1) * v_rows]), NT))
    every = jnp.concatenate(parts, axis=1)
    coupling = jnp.zeros((rank, slots), F32)
    for c in range(local):
        coupling = coupling + jnp.where(col_of == c, every[c * rank : (c + 1) * rank], 0.0)
    high, low = (part_.astype(F32) for part_ in split(coupling))

    def place(xo):
        for zo in range(zs):
            dest = peer_z(zo) * xs + (x + xo) % xs
            for c in range(local):
                hit = row_of == dest * local + c
                at = pl.ds((zo * local + c) * rank, rank)
                w_high[xo, at, :] = jnp.where(hit, high, 0.0).astype(BF16)
                w_low[xo, at, :] = jnp.where(hit, low, 0.0).astype(BF16)

    for xo in range(1, xs):
        place(xo)

    def contribute(xo, piece):
        at = columns(piece)
        out = dot3((w_high[xo], w_low[xo]), (u_high[:, at], u_low[:, at]), NN)
        for h, q in enumerate(piece):
            part[xo, q] = out[:, h * WIDTH : (h + 1) * WIDTH]

    def runs(q):
        if q in pieces[-1]:
            return [(k, n) for k, n in ((team, zs - team), (1, team - 1)) if n]
        return [(1, zs - 1)]

    def x_copy(xo, q, run):
        k, n = run
        at = pl.ds(k * own_rows, n * own_rows)
        return pltpu.make_async_remote_copy(
            src_ref=part.at[xo, q, at],
            dst_ref=got_x.at[xo - 1, q, at],
            send_sem=x_send.at[xo - 1, q, k],
            recv_sem=x_recv.at[xo - 1, q, k],
            device_id={"dev": z * xs + (x + xo) % xs},
            device_id_type=MESH,
        )

    def own_copy(xo, piece):
        at = (pl.ds(piece.start, len(piece)), pl.ds(0, own_rows))
        return pltpu.make_async_remote_copy(
            src_ref=part.at[xo, *at],
            dst_ref=got_x.at[xo - 1, *at],
            send_sem=x_send.at[xo - 1, piece.start, 0],
            recv_sem=x_recv.at[xo - 1, piece.start, 0],
            device_id={"dev": z * xs + (x + xo) % xs},
            device_id_type=MESH,
        )

    def block(k):
        return pl.ds(k * own_rows, own_rows)

    def lane_of(q, xo):
        return q if xo == 0 else chunks + (xo - 1) * early + q

    def mate_copy(k, q, xo=0):
        return pltpu.make_async_remote_copy(
            src_ref=part.at[xo, q, block(k)],
            dst_ref=got_mate.at[k - 1, lane_of(q, xo)],
            send_sem=m_send.at[k - 1, lane_of(q, xo)],
            recv_sem=m_recv.at[k - 1, lane_of(q, xo)],
            device_id={"dev": (first + team - 1 - seat) * xs + x},
            device_id_type=MESH,
        )

    def far_copy(k, q, xo=0):
        slot = teams - k // team - 1
        return pltpu.make_async_remote_copy(
            src_ref=part.at[xo, q, block(k)],
            dst_ref=got_far.at[slot, lane_of(q, xo)],
            send_sem=f_send.at[k - team, lane_of(q, xo)],
            recv_sem=f_recv.at[slot, lane_of(q, xo)],
            device_id={"dev": peer_z(k) * xs + x},
            device_id_type=MESH,
        )

    def hands_over(k):
        return jnp.where(first + k < zs, 0, 1) == seat

    def pass_on(hop):
        pl.semaphore_wait(relay.at[hop], near_z)
        if hop < zs - 2:
            greet(relay.at[hop + 1])

    def gather(k, q):
        total = part[0, q, block(k)]
        for xo in range(1, xs):
            if k == 0:
                for piece in loads:
                    if piece.start == q:
                        own_copy(xo, piece).wait_recv()
            else:
                for run in runs(q):
                    if k == next(o for o in order if run[0] <= o < run[0] + run[1]):
                        x_copy(xo, q, run).wait_recv()
            total = total + got_x[xo - 1, q, block(k)]
        return total

    def to_mate(k, q, xo):
        if k < team:
            mate_copy(k, q, xo).start()
        elif team > 1:
            @pl.when(hands_over(k))
            def _():
                mate_copy(k, q, xo).start()

    def to_far(k, q, xo):
        def send():
            if team > 1:
                mate_copy(k, q, xo).wait_recv()
                got = got_mate[k - 1, lane_of(q, xo)]
                part[xo, q, block(k)] = part[xo, q, block(k)] + got
            far_copy(k, q, xo).start()

        if team > 1:
            pl.when(jnp.logical_not(hands_over(k)))(send)
        else:
            send()

    def arrived(q, xo):
        got = []
        for k in range(1, team):
            mate_copy(k, q, xo).wait_recv()
            got.append(got_mate[k - 1, lane_of(q, xo)])
        for k in range(team, zs, team):
            far_copy(k, q, xo).wait_recv()
            got.append(got_far[teams - k // team - 1, lane_of(q, xo)])
        return functools.reduce(jnp.add, got)

    def along_z(piece):
        contribute(0, piece)
        for q in piece:
            for k in order:
                part[0, q, block(k)] = gather(k, q)
                to_mate(k, q, 0)
            for k in range(team, zs):
                to_far(k, q, 0)

    def load(piece):
        at = columns(piece)
        u_loads[loads.index(piece)].wait()
        u_high[:, at], u_low[:, at] = split(u_buf[:, at])

    for p, piece in enumerate(pieces):
        load(piece)
        for xo in range(1, xs):
            contribute(xo, piece)
        if p == 0:
            pl.semaphore_wait(barrier, xs - 1 + groups - 1 + near_z)
            greet(relay.at[0])
        for q in piece:
            for run in runs(q):
                for xo in range(1, xs):
                    x_copy(xo, q, run).start()
        if p == 0:
            place(0)
            if early:
                load(range(early))
                for xo in range(xs):
                    contribute(xo, range(early))
                for q in range(early):
                    for k in order:
                        for xo in range(xs):
                            to_mate(k, q, xo)
        if p == 1:
            for hop in range(zs - 1):
                pass_on(hop)
            for q in range(early):
                for k in range(team, zs):
                    for xo in range(xs):
                        to_far(k, q, xo)
        if p == len(pieces) - 1:
            for q in range(early):
                for xo in range(1, xs):
                    part[xo, q, block(0)] = part[xo, q, block(0)] + arrived(q, xo)
            for own in sorted(loads, key=lambda r: r.start):
                for xo in range(1, xs):
                    own_copy(xo, own).start()
        if p > 0:
            along_z(pieces[p - 1])
    along_z(pieces[-1])
    near_loads[1].wait()
    leaf_gram = jnp.zeros((own_rows, own_rows), F32)
    for q in range(chunks):
        at = pl.ds(q * WIDTH, WIDTH)
        near = [
            diag[c : c + 1, at] * sketch[c * rank : (c + 1) * rank, at] for c in range(local)
        ]
        total = gather(0, q) + jnp.concatenate(near, axis=0) + arrived(q, 0)
        sample[:, at] = total
        leaf_gram = leaf_gram + dot(total, total, NT, HIGHEST)

    save = pltpu.make_async_copy(sample, sample_out, load_sems.at[0])
    save.start()
    squares = [diagonal_block(leaf_gram, c, rank) for c in range(local)]
    packed = pack(functools.reduce(jnp.add, squares))
    gram[...] = packed
    grams[pl.ds(me, 1)] = packed[None]

    def g_copy(o):
        return pltpu.make_async_remote_copy(
            src_ref=gram,
            dst_ref=grams.at[me],
            send_sem=g_send.at[o - 1],
            recv_sem=g_recv.at[o - 1],
            device_id={"dev": (me + o) % members},
            device_id_type=MESH,
        )

    def r_copy(o):
        return pltpu.make_async_remote_copy(
            src_ref=group_gram,
            dst_ref=group_grams.at[my_group],
            send_sem=r_send.at[o - 1],
            recv_sem=r_recv.at[o - 1],
            device_id={"grp": (my_group + o) % groups},
            device_id_type=MESH,
        )

    for o in range(1, members):
        g_copy(o).start()

    @pl.when(me < members)
    def _():
        for c, (upper, inverse) in enumerate(factor(squares)):
            uppers[c] = upper
            squares_out[local + c] = inverse * math.sqrt(leaf_rows)

    for o in range(1, members):
        g_copy(o).wait_recv()
    packed_group = functools.reduce(jnp.add, [grams[i] for i in range(members)])
    group_gram[...] = packed_group
    group_grams[pl.ds(my_group, 1)] = packed_group[None]
    for o in range(1, groups):
        r_copy(o).start()

    @pl.when(my_group < groups)
    def _():
        ((upper, inverse),) = factor([unpack(packed_group, rank)])
        for c in range(local):
            squares_out[c] = dot(uppers[c], inverse, NT, HIGHEST) * math.sqrt(members * local)
        squares_out[2 * local] = upper * math.sqrt(groups)

    for o in range(1, groups):
        r_copy(o).wait_recv()
    packed_root = functools.reduce(jnp.add, [group_grams[i] for i in range(groups)])
    squares_out[2 * local + 1] = unpack(packed_root, rank)

    for q in range(chunks):
        for xo in range(1, xs):
            for run in runs(q) if q >= early else []:
                x_copy(xo, q, run).wait_send()
            for piece in loads:
                if piece.start == q:
                    own_copy(xo, piece).wait_send()
        for xo in range(xs if q < early else 1):
            for k in range(1, team):
                mate_copy(k, q, xo).wait_send()
            for k in range(team, zs):
                def sent(copy, k=k, q=q, xo=xo):
                    copy(k, q, xo).wait_send()

                if team > 1:
                    pl.when(hands_over(k))(functools.partial(sent, mate_copy))
                    pl.when(jnp.logical_not(hands_over(k)))(functools.partial(sent, far_copy))
                else:
                    sent(far_copy)
    for o in range(1, members):
        g_copy(o).wait_send()
    for o in range(1, groups):
        r_copy(o).wait_send()
    save.wait()


def finish(sample_hbm, squares, basis, t_leaf, t_group, sample, load_sem):
    local, rank, _ = basis.shape
    load = pltpu.make_async_copy(sample_hbm, sample, load_sem)
    load.start()
    for c in range(local):
        t_leaf[c] = squares[c]
    ((_, root_inverse),) = factor([squares[2 * local + 1]])
    t_group[0] = dot(squares[2 * local], root_inverse, NT, HIGHEST)
    load.wait()
    for c in range(local):
        basis[c] = dot(squares[local + c], sample[c * rank : (c + 1) * rank], NN, HIGHEST)


def body(u_blocks, v_blocks, sketch, near_diag, block_row, col_count):
    blocks, rank, leaf_rows = u_blocks.shape
    local = sketch.shape[0]
    members = lax.axis_size("dev")
    groups = lax.axis_size("grp")
    xs = max(d for d in range(1, members + 1) if members % d == 0 and d * d <= members)
    zs = members // xs
    team = 2 if zs % 2 == 0 else 1
    chunks = leaf_rows // WIDTH
    early = early_of(chunks, xs, zs)
    lanes = chunks + (xs - 1) * early
    slots = blocks * rank
    own = local * rank
    vmem = pl.BlockSpec(memory_space=pltpu.VMEM)
    hbm = pl.BlockSpec(memory_space=pl.ANY)
    dma = pltpu.SemaphoreType.DMA
    sample, squares = pl.pallas_call(
        functools.partial(kernel, xs, local),
        out_shape=(
            jax.ShapeDtypeStruct((own, leaf_rows), F32),
            jax.ShapeDtypeStruct((2 * local + 2, rank, rank), F32),
        ),
        in_specs=[hbm] * 6,
        out_specs=(hbm, vmem),
        scratch_shapes=[
            pltpu.SMEM((blocks,), jnp.int32),
            pltpu.SMEM((local,), jnp.int32),
            pltpu.VMEM((own, leaf_rows), F32),
            pltpu.VMEM((local, leaf_rows), F32),
            pltpu.VMEM((slots, leaf_rows), F32),
            pltpu.VMEM((slots, leaf_rows), F32),
            pltpu.VMEM((slots, leaf_rows), BF16),
            pltpu.VMEM((slots, leaf_rows), BF16),
            pltpu.VMEM((xs, zs * own, slots), BF16),
            pltpu.VMEM((xs, zs * own, slots), BF16),
            pltpu.VMEM((xs, chunks, zs * own, WIDTH), F32),
            pltpu.VMEM((max(xs - 1, 1), chunks, zs * own, WIDTH), F32),
            pltpu.VMEM((max(zs - 1, 1), lanes, own, WIDTH), F32),
            pltpu.VMEM((max(zs // team - 1, 1), lanes, own, WIDTH), F32),
            pltpu.VMEM((own, leaf_rows), F32),
            pltpu.VMEM((8, rank * rank // 8), F32),
            pltpu.VMEM((members, 8, rank * rank // 8), F32),
            pltpu.VMEM((8, rank * rank // 8), F32),
            pltpu.VMEM((groups, 8, rank * rank // 8), F32),
            pltpu.VMEM((local, rank, rank), F32),
            dma((5 + V_PARTS + len(pieces_of(chunks, early)),)),
            dma((max(xs - 1, 1), chunks, zs)),
            dma((max(xs - 1, 1), chunks, zs)),
            dma((max(zs - 1, 1), lanes)),
            dma((max(zs - 1, 1), lanes)),
            dma((max(zs - team, 1), lanes)),
            dma((max(zs // team - 1, 1), lanes)),
            dma((members - 1,)),
            dma((members - 1,)),
            dma((groups - 1,)),
            dma((groups - 1,)),
            pltpu.SemaphoreType.REGULAR((max(zs - 1, 1),)),
        ],
        compiler_params=pltpu.CompilerParams(
            collective_id=0, has_side_effects=True, vmem_limit_bytes=60 * 1024 * 1024
        ),
    )(
        u_blocks.reshape(slots, leaf_rows),
        v_blocks.reshape(slots, leaf_rows),
        sketch.reshape(own, leaf_rows),
        near_diag,
        block_row,
        col_count,
    )
    return pl.pallas_call(
        finish,
        out_shape=(
            jax.ShapeDtypeStruct((local, rank, leaf_rows), F32),
            jax.ShapeDtypeStruct((local, rank, rank), F32),
            jax.ShapeDtypeStruct((1, rank, rank), F32),
        ),
        in_specs=[hbm, vmem],
        out_specs=(vmem, vmem, vmem),
        scratch_shapes=[pltpu.VMEM((own, leaf_rows), F32), dma],
    )(sample, squares)


def solution(mesh):
    in_specs = (
        P(("grp", "dev"), None, None),
        P(("grp", "dev"), None, None),
        P(("grp", "dev"), None, None),
        P(("grp", "dev"), None),
        P(("grp", "dev")),
        P(("grp", "dev")),
    )
    out_specs = (P(("grp", "dev"), None, None), P(("grp", "dev"), None, None), P("grp", None, None))
    return jax.shard_map(body, mesh=mesh, in_specs=in_specs, out_specs=out_specs, check_vma=False)
```

```python
import functools
import math

import jax
import jax.numpy as jnp
from jax import lax
from jax.experimental import pallas as pl
from jax.experimental.pallas import tpu as pltpu
from jax.sharding import PartitionSpec as P

F32 = jnp.float32
BF16 = jnp.bfloat16
MESH = pl.DeviceIdType.MESH
HIGHEST = lax.Precision.HIGHEST
NN = (((1,), (0,)), ((), ()))
NT = (((1,), (1,)), ((), ()))
WIDTH = 128
PAIR = 2
V_PARTS = 1
PIVOTS = 16
LAG = 1


def dot(a, b, dims, precision=None):
    return lax.dot_general(a, b, dims, precision=precision, preferred_element_type=F32)


def split(x):
    high = x.astype(BF16)
    return high, (x - high.astype(F32)).astype(BF16)


def dot3(a, b, dims):
    (ah, al), (bh, bl) = a, b
    return dot(ah, bh, dims) + dot(ah, bl, dims) + dot(al, bh, dims)


def dot3_stacked(a, b, dims):
    (high, rest), (bh, bl) = a, b
    rows = high.shape[0]
    both = dot(jnp.concatenate([high, rest], axis=0), bh, dims)
    return both[:rows] + both[rows:] + dot(high, bl, dims)


def pack(square):
    rank = square.shape[0]
    return jnp.concatenate([square[i : i + 8] for i in range(0, rank, 8)], axis=1)


def unpack(packed, rank):
    return jnp.concatenate([packed[:, i * rank : (i + 1) * rank] for i in range(rank // 8)], axis=0)


def diagonal_block(square, c, rank):
    at = slice(c * rank, (c + 1) * rank)
    return square[at, at]


def factor(grams):
    rank = grams[0].shape[0]
    rows = lax.broadcasted_iota(jnp.int32, (rank, 2 * rank), 0)
    lanes = lax.broadcasted_iota(jnp.int32, (rank, 2 * rank), 1)
    eye = (
        lax.broadcasted_iota(jnp.int32, (rank, rank), 0)
        == lax.broadcasted_iota(jnp.int32, (rank, rank), 1)
    ).astype(F32)
    state = [jnp.concatenate([g, eye], axis=1) for g in grams]
    for j in range(0, rank, PIVOTS):
        ahead = [
            [jnp.broadcast_to(m[:, j + b : j + b + 1], m.shape) for b in range(PIVOTS)] for m in state
        ]
        for b in range(min(PIVOTS, rank - 1 - j)):
            below = rows > j + b
            for n, m in enumerate(state):
                column = ahead[n][b]
                inverse = 1.0 / column[j + b : j + b + 1]
                low = jnp.where(below, column, 0.0)
                state[n] = m - low * (m[j + b : j + b + 1] * inverse)
                for e in range(b + 1, PIVOTS):
                    ahead[n][e] = ahead[n][e] - low * (column[j + e : j + e + 1] * inverse)
    out = []
    for m in state:
        diagonal = jnp.sum(jnp.where(rows == lanes, m, 0.0), axis=1, keepdims=True)
        m = m * lax.rsqrt(diagonal)
        upper = jnp.where((rows <= lanes)[:, :rank], m[:, :rank], 0.0)
        out.append((upper, m[:, rank:]))
    return out


def pieces_of(chunks, early):
    starts = list(range(early, chunks, PAIR))
    return [range(a, b) for a, b in zip(starts, starts[1:] + [chunks])]


def early_of(chunks, xs, zs):
    return chunks // 8 if xs > 1 and zs > 2 and zs % 2 == 0 else 0


def columns(piece):
    return pl.ds(piece.start * WIDTH, len(piece) * WIDTH)


def kernel(
    xs, local, u_hbm, v_hbm, sketch_hbm, diag_hbm, row_hbm, count_hbm, sample_out, squares_out,
    block_row, col_count, sketch, diag, u_buf, v_buf, u_high, u_low, w_high, w_low, part, got_x, got_mate, got_far, sample,
    gram, grams, group_gram, group_grams, uppers,
    load_sems, x_send, x_recv, m_send, m_recv, f_send, f_recv, g_send, g_recv, r_send, r_recv, relay,
):
    slots, leaf_rows = u_buf.shape
    rank = sample.shape[0] // local
    blocks = slots // rank
    members = grams.shape[0]
    groups = group_grams.shape[0]
    zs = members // xs
    chunks = leaf_rows // WIDTH
    own_rows = local * rank
    me = lax.axis_index("dev")
    my_group = lax.axis_index("grp")
    z, x = me // xs, me % xs

    early = early_of(chunks, xs, zs)
    pieces = pieces_of(chunks, early)
    loads = pieces + ([range(early)] if early else [])
    loads = loads[:1] + loads[len(pieces) :] + loads[1 : len(pieces)]
    near_loads = [
        pltpu.make_async_copy(sketch_hbm, sketch, load_sems.at[0]),
        pltpu.make_async_copy(diag_hbm, diag, load_sems.at[1]),
    ]
    v_rows = slots // V_PARTS
    v_loads = [
        pltpu.make_async_copy(
            v_hbm.at[pl.ds(i * v_rows, v_rows)],
            v_buf.at[pl.ds(i * v_rows, v_rows)],
            load_sems.at[2 + i],
        )
        for i in range(V_PARTS)
    ]
    u_loads = []
    for p, piece in enumerate(loads):
        at = columns(piece)
        u_loads.append(
            pltpu.make_async_copy(
                u_hbm.at[:, at], u_buf.at[:, at], load_sems.at[4 + V_PARTS + p]
            )
        )
    index_loads = [
        pltpu.make_async_copy(row_hbm, block_row, load_sems.at[2 + V_PARTS]),
        pltpu.make_async_copy(count_hbm, col_count, load_sems.at[3 + V_PARTS]),
    ]
    for load in index_loads + near_loads[:1] + v_loads + u_loads[:1] + u_loads[1:] + near_loads[1:]:
        load.start()
    barrier = pltpu.get_barrier_semaphore()
    for xo in range(1, xs):
        partner = z * xs + (x + xo) % xs
        pl.semaphore_signal(barrier, inc=1, device_id={"dev": partner}, device_id_type=MESH)
    for o in range(1, groups):
        pl.semaphore_signal(
            barrier, inc=1, device_id={"grp": (my_group + o) % groups}, device_id_type=MESH
        )

    def greet(semaphore):
        @pl.when(z > 0)
        def _():
            pl.semaphore_signal(
                semaphore, inc=1, device_id={"dev": me - xs}, device_id_type=MESH
            )

        @pl.when(z < zs - 1)
        def _():
            pl.semaphore_signal(
                semaphore, inc=1, device_id={"dev": me + xs}, device_id_type=MESH
            )

    team = 2 if zs % 2 == 0 else 1
    first, seat = z // team * team, z % team
    teams = zs // team

    def peer_z(k):
        if k == 0:
            return z
        if k < team:
            return first + (seat + k) % team
        return (first + k) % zs

    order = list(range(team, zs)) + list(range(1, team))
    near_z = jnp.where(z > 0, 1, 0) + jnp.where(z < zs - 1, 1, 0)
    greet(barrier)

    for load in index_loads:
        load.wait()
    lane = lax.broadcasted_iota(jnp.int32, (1, slots), 1)
    row_of = jnp.zeros((1, slots), jnp.int32)
    slot_of = jnp.zeros((1, slots), jnp.int32)
    for s in range(blocks):
        row_of = jnp.where(lane >= s * rank, block_row[s], row_of)
        slot_of = jnp.where(lane >= s * rank, s, slot_of)
    col_of = jnp.zeros((1, slots), jnp.int32)
    end = 0
    for c in range(local):
        end = end + col_count[c]
        col_of = col_of + jnp.where(slot_of >= end, 1, 0)

    near_loads[0].wait()
    sketch_parts = split(sketch[...])
    parts = []
    for i in range(V_PARTS):
        v_loads[i].wait()
        parts.append(dot3_stacked(sketch_parts, split(v_buf[i * v_rows : (i + 1) * v_rows]), NT))
    every = jnp.concatenate(parts, axis=1)
    coupling = jnp.zeros((rank, slots), F32)
    for c in range(local):
        coupling = coupling + jnp.where(col_of == c, every[c * rank : (c + 1) * rank], 0.0)
    high, low = (part_.astype(F32) for part_ in split(coupling))

    def place(xo):
        for zo in range(zs):
            dest = peer_z(zo) * xs + (x + xo) % xs
            for c in range(local):
                hit = row_of == dest * local + c
                at = pl.ds((zo * local + c) * rank, rank)
                w_high[xo, at, :] = jnp.where(hit, high, 0.0).astype(BF16)
                w_low[xo, at, :] = jnp.where(hit, low, 0.0).astype(BF16)

    for xo in range(1, xs):
        place(xo)

    def contribute(xo, piece):
        at = columns(piece)
        out = dot3((w_high[xo], w_low[xo]), (u_high[:, at], u_low[:, at]), NN)
        for h, q in enumerate(piece):
            part[xo, q] = out[:, h * WIDTH : (h + 1) * WIDTH]

    def runs(q):
        if q in pieces[-1]:
            return [(k, n) for k, n in ((team, zs - team), (1, team - 1)) if n]
        return [(1, zs - 1)]

    def x_copy(xo, q, run):
        k, n = run
        at = pl.ds(k * own_rows, n * own_rows)
        return pltpu.make_async_remote_copy(
            src_ref=part.at[xo, q, at],
            dst_ref=got_x.at[xo - 1, q, at],
            send_sem=x_send.at[xo - 1, q, k],
            recv_sem=x_recv.at[xo - 1, q, k],
            device_id={"dev": z * xs + (x + xo) % xs},
            device_id_type=MESH,
        )

    def own_copy(xo, piece):
        at = (pl.ds(piece.start, len(piece)), pl.ds(0, own_rows))
        return pltpu.make_async_remote_copy(
            src_ref=part.at[xo, *at],
            dst_ref=got_x.at[xo - 1, *at],
            send_sem=x_send.at[xo - 1, piece.start, 0],
            recv_sem=x_recv.at[xo - 1, piece.start, 0],
            device_id={"dev": z * xs + (x + xo) % xs},
            device_id_type=MESH,
        )

    def block(k):
        return pl.ds(k * own_rows, own_rows)

    def lane_of(q, xo):
        return q if xo == 0 else chunks + (xo - 1) * early + q

    def mate_copy(k, q, xo=0):
        return pltpu.make_async_remote_copy(
            src_ref=part.at[xo, q, block(k)],
            dst_ref=got_mate.at[k - 1, lane_of(q, xo)],
            send_sem=m_send.at[k - 1, lane_of(q, xo)],
            recv_sem=m_recv.at[k - 1, lane_of(q, xo)],
            device_id={"dev": (first + team - 1 - seat) * xs + x},
            device_id_type=MESH,
        )

    def far_copy(k, q, xo=0):
        slot = teams - k // team - 1
        return pltpu.make_async_remote_copy(
            src_ref=part.at[xo, q, block(k)],
            dst_ref=got_far.at[slot, lane_of(q, xo)],
            send_sem=f_send.at[k - team, lane_of(q, xo)],
            recv_sem=f_recv.at[slot, lane_of(q, xo)],
            device_id={"dev": peer_z(k) * xs + x},
            device_id_type=MESH,
        )

    def hands_over(k):
        return jnp.where(first + k < zs, 0, 1) == seat

    def pass_on(hop):
        pl.semaphore_wait(relay.at[hop], near_z)
        if hop < zs - 2:
            greet(relay.at[hop + 1])

    def gather(k, q):
        total = part[0, q, block(k)]
        for xo in range(1, xs):
            if k == 0:
                for piece in loads:
                    if piece.start == q:
                        own_copy(xo, piece).wait_recv()
            else:
                for run in runs(q):
                    if k == next(o for o in order if run[0] <= o < run[0] + run[1]):
                        x_copy(xo, q, run).wait_recv()
            total = total + got_x[xo - 1, q, block(k)]
        return total

    def to_mate(k, q, xo):
        if k < team:
            mate_copy(k, q, xo).start()
        elif team > 1:
            @pl.when(hands_over(k))
            def _():
                mate_copy(k, q, xo).start()

    def to_far(k, q, xo):
        def send():
            if team > 1:
                mate_copy(k, q, xo).wait_recv()
                got = got_mate[k - 1, lane_of(q, xo)]
                part[xo, q, block(k)] = part[xo, q, block(k)] + got
            far_copy(k, q, xo).start()

        if team > 1:
            pl.when(jnp.logical_not(hands_over(k)))(send)
        else:
            send()

    def arrived(q, xo):
        got = []
        for k in range(1, team):
            mate_copy(k, q, xo).wait_recv()
            got.append(got_mate[k - 1, lane_of(q, xo)])
        for k in range(team, zs, team):
            far_copy(k, q, xo).wait_recv()
            got.append(got_far[teams - k // team - 1, lane_of(q, xo)])
        return functools.reduce(jnp.add, got)

    late = hands_over(team)

    def to_mate_rows(piece):
        @pl.when(late)
        def _():
            for q in piece:
                for k in range(1, team):
                    mate_copy(k, q).start()

    def along_z(p):
        contribute(0, pieces[p])
        for q in pieces[p]:
            for k in order:
                part[0, q, block(k)] = gather(k, q)
                if k >= team:
                    to_mate(k, q, 0)
                else:
                    @pl.when(jnp.logical_not(late))
                    def _(k=k, q=q):
                        mate_copy(k, q).start()
            for k in range(team, zs):
                to_far(k, q, 0)
        if p >= LAG:
            to_mate_rows(pieces[p - LAG])

    def load(piece):
        at = columns(piece)
        u_loads[loads.index(piece)].wait()
        u_high[:, at], u_low[:, at] = split(u_buf[:, at])

    for p, piece in enumerate(pieces):
        load(piece)
        for xo in range(1, xs):
            contribute(xo, piece)
        if p == 0:
            pl.semaphore_wait(barrier, xs - 1 + groups - 1 + near_z)
            greet(relay.at[0])
        for q in piece:
            for run in runs(q):
                for xo in range(1, xs):
                    x_copy(xo, q, run).start()
        if p == 0:
            place(0)
            if early:
                load(range(early))
                for xo in range(xs):
                    contribute(xo, range(early))
                for q in range(early):
                    for k in order:
                        for xo in range(xs):
                            to_mate(k, q, xo)
        if p == 1:
            for hop in range(zs - 1):
                pass_on(hop)
            for q in range(early):
                for k in range(team, zs):
                    for xo in range(xs):
                        to_far(k, q, xo)
        if p == len(pieces) - 1:
            for q in range(early):
                for xo in range(1, xs):
                    part[xo, q, block(0)] = part[xo, q, block(0)] + arrived(q, xo)
            for own in sorted(loads, key=lambda r: r.start):
                for xo in range(1, xs):
                    own_copy(xo, own).start()
        if p > 0:
            along_z(p - 1)
    along_z(len(pieces) - 1)
    for piece in pieces[max(len(pieces) - LAG, 0) :]:
        to_mate_rows(piece)
    near_loads[1].wait()
    leaf_gram = jnp.zeros((own_rows, own_rows), F32)
    for q in range(chunks):
        at = pl.ds(q * WIDTH, WIDTH)
        near = [
            diag[c : c + 1, at] * sketch[c * rank : (c + 1) * rank, at] for c in range(local)
        ]
        total = gather(0, q) + jnp.concatenate(near, axis=0) + arrived(q, 0)
        sample[:, at] = total
        leaf_gram = leaf_gram + dot(total, total, NT, HIGHEST)

    save = pltpu.make_async_copy(sample, sample_out, load_sems.at[0])
    save.start()
    squares = [diagonal_block(leaf_gram, c, rank) for c in range(local)]
    packed = pack(functools.reduce(jnp.add, squares))
    gram[...] = packed
    grams[pl.ds(me, 1)] = packed[None]

    def g_copy(o):
        return pltpu.make_async_remote_copy(
            src_ref=gram,
            dst_ref=grams.at[me],
            send_sem=g_send.at[o - 1],
            recv_sem=g_recv.at[o - 1],
            device_id={"dev": (me + o) % members},
            device_id_type=MESH,
        )

    def r_copy(o):
        return pltpu.make_async_remote_copy(
            src_ref=group_gram,
            dst_ref=group_grams.at[my_group],
            send_sem=r_send.at[o - 1],
            recv_sem=r_recv.at[o - 1],
            device_id={"grp": (my_group + o) % groups},
            device_id_type=MESH,
        )

    for o in range(1, members):
        g_copy(o).start()

    @pl.when(me < members)
    def _():
        for c, (upper, inverse) in enumerate(factor(squares)):
            uppers[c] = upper
            squares_out[local + c] = inverse * math.sqrt(leaf_rows)

    for o in range(1, members):
        g_copy(o).wait_recv()
    packed_group = functools.reduce(jnp.add, [grams[i] for i in range(members)])
    group_gram[...] = packed_group
    group_grams[pl.ds(my_group, 1)] = packed_group[None]
    for o in range(1, groups):
        r_copy(o).start()

    @pl.when(my_group < groups)
    def _():
        ((upper, inverse),) = factor([unpack(packed_group, rank)])
        for c in range(local):
            squares_out[c] = dot(uppers[c], inverse, NT, HIGHEST) * math.sqrt(members * local)
        squares_out[2 * local] = upper * math.sqrt(groups)

    for o in range(1, groups):
        r_copy(o).wait_recv()
    packed_root = functools.reduce(jnp.add, [group_grams[i] for i in range(groups)])
    squares_out[2 * local + 1] = unpack(packed_root, rank)

    for q in range(chunks):
        for xo in range(1, xs):
            for run in runs(q) if q >= early else []:
                x_copy(xo, q, run).wait_send()
            for piece in loads:
                if piece.start == q:
                    own_copy(xo, piece).wait_send()
        for xo in range(xs if q < early else 1):
            for k in range(1, team):
                mate_copy(k, q, xo).wait_send()
            for k in range(team, zs):
                def sent(copy, k=k, q=q, xo=xo):
                    copy(k, q, xo).wait_send()

                if team > 1:
                    pl.when(hands_over(k))(functools.partial(sent, mate_copy))
                    pl.when(jnp.logical_not(hands_over(k)))(functools.partial(sent, far_copy))
                else:
                    sent(far_copy)
    for o in range(1, members):
        g_copy(o).wait_send()
    for o in range(1, groups):
        r_copy(o).wait_send()
    save.wait()


def finish(sample_hbm, squares, basis, t_leaf, t_group, sample, load_sem):
    local, rank, _ = basis.shape
    load = pltpu.make_async_copy(sample_hbm, sample, load_sem)
    load.start()
    for c in range(local):
        t_leaf[c] = squares[c]
    ((_, root_inverse),) = factor([squares[2 * local + 1]])
    t_group[0] = dot(squares[2 * local], root_inverse, NT, HIGHEST)
    load.wait()
    for c in range(local):
        basis[c] = dot(squares[local + c], sample[c * rank : (c + 1) * rank], NN, HIGHEST)


def body(u_blocks, v_blocks, sketch, near_diag, block_row, col_count):
    blocks, rank, leaf_rows = u_blocks.shape
    local = sketch.shape[0]
    members = lax.axis_size("dev")
    groups = lax.axis_size("grp")
    xs = max(d for d in range(1, members + 1) if members % d == 0 and d * d <= members)
    zs = members // xs
    team = 2 if zs % 2 == 0 else 1
    chunks = leaf_rows // WIDTH
    early = early_of(chunks, xs, zs)
    lanes = chunks + (xs - 1) * early
    slots = blocks * rank
    own = local * rank
    vmem = pl.BlockSpec(memory_space=pltpu.VMEM)
    hbm = pl.BlockSpec(memory_space=pl.ANY)
    dma = pltpu.SemaphoreType.DMA
    sample, squares = pl.pallas_call(
        functools.partial(kernel, xs, local),
        out_shape=(
            jax.ShapeDtypeStruct((own, leaf_rows), F32),
            jax.ShapeDtypeStruct((2 * local + 2, rank, rank), F32),
        ),
        in_specs=[hbm] * 6,
        out_specs=(hbm, vmem),
        scratch_shapes=[
            pltpu.SMEM((blocks,), jnp.int32),
            pltpu.SMEM((local,), jnp.int32),
            pltpu.VMEM((own, leaf_rows), F32),
            pltpu.VMEM((local, leaf_rows), F32),
            pltpu.VMEM((slots, leaf_rows), F32),
            pltpu.VMEM((slots, leaf_rows), F32),
            pltpu.VMEM((slots, leaf_rows), BF16),
            pltpu.VMEM((slots, leaf_rows), BF16),
            pltpu.VMEM((xs, zs * own, slots), BF16),
            pltpu.VMEM((xs, zs * own, slots), BF16),
            pltpu.VMEM((xs, chunks, zs * own, WIDTH), F32),
            pltpu.VMEM((max(xs - 1, 1), chunks, zs * own, WIDTH), F32),
            pltpu.VMEM((max(zs - 1, 1), lanes, own, WIDTH), F32),
            pltpu.VMEM((max(zs // team - 1, 1), lanes, own, WIDTH), F32),
            pltpu.VMEM((own, leaf_rows), F32),
            pltpu.VMEM((8, rank * rank // 8), F32),
            pltpu.VMEM((members, 8, rank * rank // 8), F32),
            pltpu.VMEM((8, rank * rank // 8), F32),
            pltpu.VMEM((groups, 8, rank * rank // 8), F32),
            pltpu.VMEM((local, rank, rank), F32),
            dma((5 + V_PARTS + len(pieces_of(chunks, early)),)),
            dma((max(xs - 1, 1), chunks, zs)),
            dma((max(xs - 1, 1), chunks, zs)),
            dma((max(zs - 1, 1), lanes)),
            dma((max(zs - 1, 1), lanes)),
            dma((max(zs - team, 1), lanes)),
            dma((max(zs // team - 1, 1), lanes)),
            dma((members - 1,)),
            dma((members - 1,)),
            dma((groups - 1,)),
            dma((groups - 1,)),
            pltpu.SemaphoreType.REGULAR((max(zs - 1, 1),)),
        ],
        compiler_params=pltpu.CompilerParams(
            collective_id=0, has_side_effects=True, vmem_limit_bytes=60 * 1024 * 1024
        ),
    )(
        u_blocks.reshape(slots, leaf_rows),
        v_blocks.reshape(slots, leaf_rows),
        sketch.reshape(own, leaf_rows),
        near_diag,
        block_row,
        col_count,
    )
    return pl.pallas_call(
        finish,
        out_shape=(
            jax.ShapeDtypeStruct((local, rank, leaf_rows), F32),
            jax.ShapeDtypeStruct((local, rank, rank), F32),
            jax.ShapeDtypeStruct((1, rank, rank), F32),
        ),
        in_specs=[hbm, vmem],
        out_specs=(vmem, vmem, vmem),
        scratch_shapes=[pltpu.VMEM((own, leaf_rows), F32), dma],
    )(sample, squares)


def solution(mesh):
    in_specs = (
        P(("grp", "dev"), None, None),
        P(("grp", "dev"), None, None),
        P(("grp", "dev"), None, None),
        P(("grp", "dev"), None),
        P(("grp", "dev")),
        P(("grp", "dev")),
    )
    out_specs = (P(("grp", "dev"), None, None), P(("grp", "dev"), None, None), P("grp", None, None))
    return jax.shard_map(body, mesh=mesh, in_specs=in_specs, out_specs=out_specs, check_vma=False)
```
